128 devices in a mesh: tok: 8 (over x, core), voc: 16 (over y, z).
Axes of the slice: x: 4, y: 4, z: 4, core: 2. Of those that a mesh axis runs over, the one named last changes fastest.
Arguments:
- tokens_in: bfloat16 [1024, 4096], P(('tok', 'voc')), may hold values from -36 to 36
- gate_raw: float32 [1024, 8], P(('tok', 'voc')), may hold values from 0.05 to 1
- expert_ids: int32 [1024, 8], P(('tok', 'voc')), may hold values from 0 to 63, all different within a row; in each aligned block of 8 rows (0 to 7, 8 to 15, ...) at most 2 rows name the same one
- w_gate: bfloat16 [4096, 49152], P(None, ('tok', 'voc')), may hold values from -0.09375 to 0.09375
- w_up: bfloat16 [4096, 49152], P(None, ('tok', 'voc')), may hold values from -0.09375 to 0.09375
- w_down: bfloat16 [49152, 4096], P(('tok', 'voc')), may hold values from -0.875 to 0.875
- final_gain: float32 [4096], replicated, may hold values from 0.1 to 1.9
- teacher_head: bfloat16 [4096, 77824], P('tok', 'voc')
- student_hidden: bfloat16 [1024, 4096], P('voc', 'tok'), may hold values from -6 to 6
- student_head: bfloat16 [4096, 77824], P('tok', 'voc')
- sampled_ids: int32 [1024], P('tok'), may hold values from 0 to 77823
- token_weight: float32 [1024], P('tok'), may hold values from 2 to 32
Outputs:
- token_loss: float32 [1024], P('tok')
- hidden_grad: bfloat16 [1024, 4096], P('voc', 'tok')
The draws below stay inside these ranges and needn't reach their ends.
Inputs may be any that keep to these rules, and one draw needn't show every extreme that they name: `expert_ids`: each row names 8 different experts; in the 8 rows of one device no expert is named by more than 2 rows, a bound that some block reaches.
All inputs are finite; a program needn't handle non-finite values.
Results may differ from the reference program's by a relative error of at most 0.01375.
Values may be sent and summed in bfloat16 or wider, within the bound.
A program may use at most 128 MiB of HBM per device.

```python
import math
from functools import partial
import jax
import jax.numpy as jnp
import numpy as np
from jax import lax

D = 4096
FF = 768
TOP = 8
VOCAB = 77824
TOK_DEV = 8
EXPERTS = 64
TOKENS = 1024
CAP = 2
N_TOK = 8
N_VOC = 16


teacher_strength = (120.0, 220.0, 320.0)


student_strength = (110.0, 210.0, 310.0)


def aligned_setup(key):
    sign_bits = jax.random.bernoulli(jax.random.fold_in(key, 1), 0.5, (3, D))
    directions = jnp.where(sign_bits, 1.0, -1.0).astype(jnp.float32) * D ** (-0.5)
    row_picks = jax.random.randint(jax.random.fold_in(key, 2), (3, 2), 0, TOKENS)
    col_picks = jax.random.randint(jax.random.fold_in(key, 3), (3,), 0, VOCAB - 1)
    return (directions, row_picks, col_picks)


def draw_tokens_in(key, part):
    normal_part = jax.random.truncated_normal(jax.random.fold_in(key, 10), -6.0, 6.0, (TOKENS, D), jnp.float32)
    row_range = math.log(2.0)
    column_scale = jnp.exp(jax.random.uniform(jax.random.fold_in(key, 11), (1, D), jnp.float32, math.log(0.3), math.log(3.0)))
    row_scale = jnp.exp(jax.random.uniform(jax.random.fold_in(key, 12), (TOKENS, 1), jnp.float32, -row_range, row_range))
    values = normal_part * column_scale * row_scale
    directions, row_picks, col_picks = aligned_setup(jax.random.fold_in(key, 100))
    for strength_index in range(3):
        for copy_index in range(2):
            values = values.at[row_picks[strength_index, copy_index]].set(directions[strength_index] * (1.5 * D ** 0.5))
    return values.astype(jnp.bfloat16)


def draw_teacher_head(key, part):
    values = jax.random.truncated_normal(jax.random.fold_in(key, 20), -6.0, 6.0, (D, VOCAB), jnp.float32) * (3.0 * D ** (-0.5))
    directions, row_picks, col_picks = aligned_setup(jax.random.fold_in(key, 100))
    for strength_index in range(3):
        strength = teacher_strength[strength_index]
        values = values.at[:, col_picks[strength_index]].set(directions[strength_index] * (strength * D ** (-0.5)))
        values = values.at[:, col_picks[strength_index] + 1].set(directions[strength_index] * ((strength - 2.5) * D ** (-0.5)))
    return values.astype(jnp.bfloat16)


def draw_student_hidden(key, part):
    values = jax.random.truncated_normal(jax.random.fold_in(key, 30), -6.0, 6.0, (TOKENS, D), jnp.float32)
    directions, row_picks, col_picks = aligned_setup(jax.random.fold_in(key, 100))
    for strength_index in range(3):
        for copy_index in range(2):
            values = values.at[row_picks[strength_index, copy_index]].set(directions[strength_index] * (4.0 * D ** 0.5))
    return values.astype(jnp.bfloat16)


def draw_student_head(key, part):
    values = jax.random.truncated_normal(jax.random.fold_in(key, 40), -6.0, 6.0, (D, VOCAB), jnp.float32) * (3.0 * D ** (-0.5))
    directions, row_picks, col_picks = aligned_setup(jax.random.fold_in(key, 100))
    for strength_index in range(3):
        strength = student_strength[strength_index]
        values = values.at[:, col_picks[strength_index]].set(directions[strength_index] * (strength * 0.25 * D ** (-0.5)))
        values = values.at[:, col_picks[strength_index] + 1].set(directions[strength_index] * ((strength - 2.0) * 0.25 * D ** (-0.5)))
    return values.astype(jnp.bfloat16)


def set_ends(array, rng, low, high):
    shape = array.shape
    place = [jax.random.randint(jax.random.fold_in(rng, axis), (), 0, shape[axis]) for axis in range(len(shape))]
    array = array.at[tuple(place)].set(low)
    longest = shape.index(max(shape))
    place[longest] = (place[longest] + 1) % shape[longest]
    return array.at[tuple(place)].set(high)


def block_levels(stream_key, extent, split, low, top_value):
    gain, own = 1.0, jax.random.fold_in(stream_key, 6)
    for axis_at, blocks in split:
        heights = jnp.exp(jax.random.uniform(jax.random.fold_in(own, axis_at), (blocks,), jnp.float32, low / len(split), top_value / len(split)))
        gain = gain * jnp.repeat(heights, extent[axis_at] // blocks).reshape([-1 if axis == axis_at else 1 for axis in range(len(extent))])
    return gain


def skewed_wide(key, dims, count, slope):
    weights = [min(1 << octave, count + 1 - (1 << octave)) * (1 << 20) // math.isqrt((1 << octave) ** slope) + 1 for octave in range((count + 1).bit_length()) if 1 << octave <= count]
    deviation = 1 + sum(weights) // (1 << 30)
    listing = np.cumsum(np.array([max(1, weight // deviation) for weight in weights]))
    ticket = jax.random.randint(jax.random.fold_in(key, 1), dims, 0, int(listing[len(weights) - 1]))
    start = jnp.left_shift(1, jnp.searchsorted(jnp.asarray(listing, jnp.int32), ticket, side="right").astype(jnp.int32))
    grade = start - 1 + jax.random.randint(jax.random.fold_in(key, 4), dims, 0, 1 << 30) % jnp.minimum(start, count + 1 - start)
    return jax.random.permutation(jax.random.fold_in(key, 2), count)[grade].astype(jnp.int32)


def assign_block(own_key, own, number, rows, count, top, bound, lean):
    sequence = jax.random.permutation(own_key, count)
    packed, ordinary = load_shares(count, rows * top, bound, lean, True), load_shares(count, rows * top, bound, lean, False)
    places = jnp.arange(count)

    def named(sizes, rotation):
        used = int((sizes > 0).sum())
        fixed = max(1, used // 4)
        passed = fixed + (places - fixed + rotation * (used - fixed)) % max(1, count - fixed)
        return jnp.zeros((count,), jnp.int32).at[sequence[jnp.where(places < fixed, places, passed)]].set(jnp.asarray(sizes, jnp.int32))

    sizes = jnp.where(number % 4 == 0, named(packed, number // 4), named(ordinary, number - number // 4 - 1))
    mixed = jax.random.permutation(jax.random.fold_in(own, 3), count)
    source_of, receiver = mixed[0:count // 2 * 2:2], mixed[1:count // 2 * 2:2]
    margin = jnp.minimum(sizes[source_of] - 1, bound - sizes[receiver]) // 2
    margin = jnp.where((source_of == sequence[0]) | (receiver == sequence[0]) | (sizes[receiver] == 0), 0, jnp.maximum(margin, 0))
    passed = jax.random.randint(jax.random.fold_in(own, 4), (count // 2,), 0, 1 << 20) % (margin + 1)
    sizes = sizes.at[source_of].add(-passed).at[receiver].add(passed)
    members = jnp.searchsorted(jnp.cumsum(sizes), jnp.arange(rows * top), side="right").astype(jnp.int32)
    table = members.reshape(top, rows).T
    table = table[jax.random.permutation(jax.random.fold_in(own, 1), rows)]
    rotation = jax.random.randint(jax.random.fold_in(own, 2), (rows, 1), 0, top)
    return jnp.take_along_axis(table, (jnp.arange(top)[None, :] + rotation) % top, axis=1)


def load_shares(number_of, total, most, slope, full):
    loads = [(1 << 20) // math.isqrt(standing ** slope) + 1 for standing in range(1, number_of + 1)]
    largest = most if full else min(most, max(-(-total // number_of), total * loads[0] // sum(loads)))
    least = 1 if total - largest >= number_of - 1 else 0
    given, rest = [largest] + [least] * (number_of - 1), total - largest - least * (number_of - 1)
    while rest > 0:
        free = [i for i in range(1, number_of) if given[i] < largest] or [i for i in range(1, number_of) if given[i] < most]
        pool, remaining = sum([loads[i] for i in free]), rest
        for i in free:
            extra = min(most - given[i], max(1, remaining * loads[i] // pool), rest)
            given[i] = given[i] + extra
            rest = rest - extra
    return np.array(given)


def noise(key, dims, scale, most, split=(), held_as=jnp.bfloat16):
    drawn = scale * jax.random.normal(key, dims, jnp.float32)
    if split:
        drawn = drawn * block_levels(key, dims, split, -0.22, 0.18)
    return jnp.clip(drawn, -most, most).astype(held_as)


def setup_inputs(seed: int = 0) -> dict:
    seeds = jax.random.split(jax.random.key(seed), 13)
    tokens_in = draw_tokens_in(jax.random.fold_in(seeds[12], 71), 0)
    gate_raw = jnp.clip(jnp.exp(math.log(1.0) - 2.9957323 * jax.random.uniform(seeds[1], (TOKENS, TOP), jnp.float32) ** block_levels(seeds[1], (TOKENS, TOP), ((0, 128),), -0.2, 0.2)), 0.05, 1.0)
    expert_ids_keys = jax.random.split(jax.random.fold_in(seeds[2], 1), TOKENS // TOK_DEV)
    expert_ids_turns = jax.random.permutation(jax.random.fold_in(seeds[2], 3), TOKENS // TOK_DEV)
    expert_ids = jax.vmap(lambda own, number: assign_block(jax.random.fold_in(seeds[2], 2), own, number, TOK_DEV, EXPERTS, TOP, CAP, 2))(expert_ids_keys, expert_ids_turns).reshape((TOKENS, TOP))
    w_gate = noise(seeds[3], (D, EXPERTS * FF), D ** -0.5, 0.09375, ((1, 128),))
    w_up = noise(seeds[4], (D, EXPERTS * FF), D ** -0.5, 0.09375, ((1, 128),))
    w_down = noise(seeds[5], (EXPERTS * FF, D), (FF // 16) ** -0.5, 0.875, ((0, 128),))
    final_gain = jnp.clip(1.0 + 0.18 * jax.random.normal(seeds[6], (D,), jnp.float32), 0.1, 1.9)
    teacher_head = draw_teacher_head(jax.random.fold_in(seeds[12], 71), 0)
    student_hidden = draw_student_hidden(jax.random.fold_in(seeds[12], 71), 0)
    student_head = draw_student_head(jax.random.fold_in(seeds[12], 71), 0)
    sampled_ids = set_ends(skewed_wide(seeds[10], (TOKENS,), VOCAB, 2), jax.random.fold_in(seeds[10], 3), 0, VOCAB - 1).astype(jnp.int32)
    token_weight = jnp.clip(jnp.exp(math.log(32.0) - 2.7725887 * jax.random.uniform(seeds[11], (TOKENS,), jnp.float32) ** block_levels(seeds[11], (TOKENS,), ((0, 8),), -0.2, 0.2)), 2.0, 32.0)
    return {"tokens_in": tokens_in, "gate_raw": gate_raw, "expert_ids": expert_ids, "w_gate": w_gate, "w_up": w_up, "w_down": w_down, "final_gain": final_gain, "teacher_head": teacher_head, "student_hidden": student_hidden, "student_head": student_head, "sampled_ids": sampled_ids, "token_weight": token_weight}


def route_tables(expert_ids, gate_raw, experts, capacity):
    rows_here, top_k = expert_ids.shape
    flat_ids = expert_ids.reshape(-1)
    one_hot = (flat_ids[:, None] == jnp.arange(experts, dtype=jnp.int32)[None, :]).astype(jnp.int32)
    earlier = jnp.cumsum(one_hot, axis=0, dtype=jnp.int32) - one_hot
    slot_of = lax.optimization_barrier(jnp.sum(earlier * one_hot, axis=1, dtype=jnp.int32))
    where_to = (flat_ids * capacity + slot_of).reshape(rows_here, top_k)
    columns = jnp.arange(experts * capacity, dtype=jnp.int32)
    matched = where_to[:, :, None] == columns[None, None, :]
    shares = gate_raw / lax.optimization_barrier(jnp.sum(gate_raw, axis=1, keepdims=True))
    combine_table = lax.optimization_barrier(jnp.sum(jnp.where(matched, shares[:, :, None], 0.0), axis=1))
    dispatch_table = jnp.transpose(jnp.any(matched, axis=1)).astype(jnp.bfloat16)
    return (dispatch_table, combine_table)

def expert_half(expert_rows, w_gate, w_up, w_down, first_unit, half_units):
    gate_cols = lax.dynamic_slice_in_dim(w_gate, first_unit, half_units, 1)
    up_cols = lax.dynamic_slice_in_dim(w_up, first_unit, half_units, 1)
    down_rows = lax.dynamic_slice_in_dim(w_down, first_unit, half_units, 0)
    gate_part = jnp.dot(expert_rows, gate_cols, preferred_element_type=jnp.float32)
    up_part = jnp.dot(expert_rows, up_cols, preferred_element_type=jnp.float32)
    hidden_units = (jax.nn.silu(gate_part) * up_part).astype(jnp.bfloat16)
    partial_out = jnp.dot(hidden_units, down_rows, preferred_element_type=jnp.float32).astype(jnp.bfloat16)
    return lax.optimization_barrier(partial_out).astype(jnp.float32)

def head_logits(hidden, head_weight):
    return jnp.dot(hidden, head_weight, preferred_element_type=jnp.float32)

def reference(tokens_in, gate_raw, expert_ids, w_gate, w_up, w_down, final_gain, teacher_head, student_hidden, student_head, sampled_ids, token_weight):
    devices = N_TOK * N_VOC
    half_units = FF // 2
    tables = jax.vmap(partial(route_tables, experts=EXPERTS, capacity=CAP))
    dispatch_table, combine_table = tables(expert_ids.reshape(devices, TOK_DEV, TOP), gate_raw.reshape(devices, TOK_DEV, TOP))
    blocks = tokens_in.reshape(devices, TOK_DEV, D)
    sent_rows = jnp.einsum('skt,std->skd', dispatch_table.astype(jnp.float32), blocks.astype(jnp.float32)).astype(jnp.bfloat16)
    by_expert = jnp.transpose(sent_rows.reshape(devices, EXPERTS, CAP, D), (1, 0, 2, 3)).reshape(EXPERTS, devices * CAP, D)

    def one_expert(expert_index):
        expert_rows = by_expert[expert_index]
        first_unit = expert_index * FF
        lower_half = expert_half(expert_rows, w_gate, w_up, w_down, first_unit, half_units)
        upper_half = expert_half(expert_rows, w_gate, w_up, w_down, first_unit + half_units, half_units)
        return lower_half + upper_half
    outputs = lax.map(one_expert, jnp.arange(EXPERTS, dtype=jnp.int32))
    returned = jnp.transpose(outputs.reshape(EXPERTS, devices, CAP, D), (1, 0, 2, 3)).reshape(devices, EXPERTS * CAP, D)
    expert_mix = jnp.einsum('stk,skd->std', combine_table, returned, precision=lax.Precision.HIGHEST).reshape(TOKENS, D)
    residual_sum = tokens_in.astype(jnp.float32) + expert_mix
    inverse = lax.rsqrt(lax.optimization_barrier(jnp.mean(residual_sum * residual_sum, axis=1, keepdims=True)) + 1e-06)
    normed = (residual_sum * inverse * final_gain[None, :]).astype(jnp.bfloat16)
    teacher_logits = head_logits(normed, teacher_head)
    student_logits = head_logits(student_hidden, student_head)
    teacher_max = lax.optimization_barrier(jnp.max(teacher_logits, axis=1))
    student_max = lax.optimization_barrier(jnp.max(student_logits, axis=1))
    teacher_norm = teacher_max + jnp.log(lax.optimization_barrier(jnp.sum(jnp.exp(teacher_logits - teacher_max[:, None]), axis=1)))
    student_norm = student_max + jnp.log(lax.optimization_barrier(jnp.sum(jnp.exp(student_logits - student_max[:, None]), axis=1)))
    student_prob = jnp.exp(student_logits - student_norm[:, None])
    differ = student_logits - teacher_logits
    expect = lax.optimization_barrier(jnp.sum(student_prob * differ, axis=1))
    picked = sampled_ids[:, None] == jnp.arange(VOCAB, dtype=jnp.int32)[None, :]
    picked_s = lax.optimization_barrier(jnp.sum(jnp.where(picked, student_logits, 0.0), axis=1))
    picked_t = lax.optimization_barrier(jnp.sum(jnp.where(picked, teacher_logits, 0.0), axis=1))
    token_loss = expect - student_norm + teacher_norm + (picked_s - student_norm) - (picked_t - teacher_norm)
    logit_grad = (token_weight[:, None] * (student_prob * (differ - expect[:, None]) + picked.astype(jnp.float32) - student_prob)).astype(jnp.bfloat16)
    hidden_grad = lax.dot_general(logit_grad, student_head, (((1,), (1,)), ((), ())), preferred_element_type=jnp.float32).astype(jnp.bfloat16)
    return (token_loss, hidden_grad)
```

```python
import functools
import jax
import jax.numpy as jnp
from jax import lax
from jax.experimental import pallas as pl
from jax.experimental.pallas import tpu as pltpu
from jax.sharding import PartitionSpec as P

MESH = pl.DeviceIdType.MESH


def route_tables(expert_ids, gate_raw, experts, capacity):
    rows_here, top_k = expert_ids.shape
    flat_ids = expert_ids.reshape(-1)
    one_hot = (flat_ids[:, None] == jnp.arange(experts, dtype=jnp.int32)[None, :]).astype(jnp.int32)
    earlier = jnp.cumsum(one_hot, axis=0, dtype=jnp.int32) - one_hot
    slot_of = jnp.sum(earlier * one_hot, axis=1, dtype=jnp.int32)
    where_to = (flat_ids * capacity + slot_of).reshape(rows_here, top_k)
    columns = jnp.arange(experts * capacity, dtype=jnp.int32)
    matched = where_to[:, :, None] == columns[None, None, :]
    shares = gate_raw / jnp.sum(gate_raw, axis=1, keepdims=True)
    combine_table = jnp.sum(jnp.where(matched, shares[:, :, None], 0.0), axis=1)
    dispatch_table = jnp.transpose(jnp.any(matched, axis=1)).astype(jnp.bfloat16)
    return (dispatch_table, combine_table)


def gather_kernel(n, x_ref, out_ref, send_sem, recv_sem, own_sem):
    t, me = lax.axis_index("tok"), lax.axis_index("voc")
    barrier = pltpu.get_barrier_semaphore()

    @pl.loop(1, n)
    def _(k):
        pl.semaphore_signal(
            barrier, inc=1, device_id=(t, lax.rem(me + k, n)), device_id_type=MESH
        )

    pl.semaphore_wait(barrier, n - 1)

    def copy(k):
        return pltpu.make_async_remote_copy(
            src_ref=x_ref,
            dst_ref=out_ref.at[me],
            send_sem=send_sem.at[k],
            recv_sem=recv_sem.at[k],
            device_id=(t, lax.rem(me + k, n)),
            device_id_type=MESH,
        )

    @pl.loop(1, n)
    def _(k):
        copy(k).start()

    own = pltpu.make_async_copy(x_ref, out_ref.at[me], own_sem)
    own.start()
    own.wait()

    @pl.loop(1, n)
    def _(k):
        pltpu.make_async_remote_copy(
            src_ref=x_ref,
            dst_ref=out_ref.at[lax.rem(me - k + n, n)],
            send_sem=send_sem.at[k],
            recv_sem=recv_sem.at[k],
            device_id=(t, lax.rem(me + k, n)),
            device_id_type=MESH,
        ).wait()


def voc_gather(x, n, collective_id):
    return pl.pallas_call(
        functools.partial(gather_kernel, n),
        out_shape=jax.ShapeDtypeStruct((n,) + x.shape, x.dtype),
        in_specs=[pl.BlockSpec(memory_space=pltpu.VMEM)],
        out_specs=pl.BlockSpec(memory_space=pltpu.VMEM),
        scratch_shapes=[
            pltpu.SemaphoreType.DMA((n,)),
            pltpu.SemaphoreType.DMA((n,)),
            pltpu.SemaphoreType.DMA,
        ],
        compiler_params=pltpu.CompilerParams(collective_id=collective_id, has_side_effects=True),
    )(x)


def per_device(
    tokens_in,
    gate_raw,
    expert_ids,
    w_gate,
    w_up,
    w_down,
    final_gain,
    teacher_head,
    student_hidden,
    student_head,
    sampled_ids,
    token_weight,
):
    tok_count = lax.axis_size("tok")
    voc_count = lax.axis_size("voc")
    experts = tok_count * voc_count // 2
    rows_here, top_k = expert_ids.shape
    model_width = tokens_in.shape[1]
    capacity = max(2, 2 * rows_here * top_k // experts)
    dispatch_table, combine_table = route_tables(expert_ids, gate_raw, experts, capacity)
    dispatched = jnp.dot(dispatch_table, tokens_in, preferred_element_type=jnp.float32).astype(
        jnp.bfloat16
    )
    outgoing = jnp.repeat(dispatched.reshape(experts, capacity, model_width), 2, axis=0)
    student_all = voc_gather(student_hidden, voc_count, 1).reshape(-1, student_hidden.shape[1])
    student_part = jnp.dot(student_all, student_head, preferred_element_type=jnp.float32)
    outgoing, student_part = lax.optimization_barrier((outgoing, student_part))
    student_logits = lax.psum_scatter(student_part, "tok", scatter_dimension=0, tiled=True)
    arrived = lax.all_to_all(outgoing, ("tok", "voc"), split_axis=0, concat_axis=0, tiled=True)
    expert_rows = arrived.reshape(2 * experts * capacity, model_width)
    gate_part = jnp.dot(expert_rows, w_gate, preferred_element_type=jnp.float32)
    up_part = jnp.dot(expert_rows, w_up, preferred_element_type=jnp.float32)
    hidden_units = (jax.nn.silu(gate_part) * up_part).astype(jnp.bfloat16)
    partial_out = (
        jnp.dot(hidden_units, w_down, preferred_element_type=jnp.float32)
        .astype(jnp.bfloat16)
        .reshape(2 * experts, capacity, model_width)
    )
    returned = lax.all_to_all(partial_out, ("tok", "voc"), split_axis=0, concat_axis=0, tiled=True)
    pair_sum = jnp.sum(
        returned.astype(jnp.float32).reshape(experts, 2, capacity, model_width), axis=1
    ).reshape(experts * capacity, model_width)
    expert_mix = jnp.dot(combine_table, pair_sum, precision=lax.Precision.HIGHEST)
    residual_sum = tokens_in.astype(jnp.float32) + expert_mix
    inverse = lax.rsqrt(jnp.mean(residual_sum * residual_sum, axis=1, keepdims=True) + 1e-06)
    normed = (residual_sum * inverse * final_gain[None, :]).astype(jnp.bfloat16)
    tok_rows = voc_gather(normed, voc_count, 2).reshape(-1, model_width)
    teacher_cols = lax.all_to_all(tok_rows, "tok", split_axis=1, concat_axis=0, tiled=True)
    vocab_local = teacher_head.shape[1]
    teacher_part = jnp.dot(teacher_cols, teacher_head, preferred_element_type=jnp.float32)
    teacher_part, student_logits = lax.optimization_barrier(
        (teacher_part.astype(jnp.bfloat16), student_logits)
    )
    teacher_logits = lax.psum_scatter(
        teacher_part, "tok", scatter_dimension=0, tiled=True
    ).astype(jnp.float32)
    differ = student_logits - teacher_logits
    vocab_start = lax.axis_index("voc") * vocab_local
    picked = sampled_ids[:, None] - vocab_start == jnp.arange(vocab_local, dtype=jnp.int32)[None, :]
    local_tmax = jnp.max(teacher_logits, axis=1)
    local_smax = jnp.max(student_logits, axis=1)
    student_exp = jnp.exp(student_logits - local_smax[:, None])
    stats = jnp.stack(
        [
            local_tmax,
            local_smax,
            jnp.sum(jnp.exp(teacher_logits - local_tmax[:, None]), axis=1),
            jnp.sum(student_exp, axis=1),
            jnp.sum(student_exp * differ, axis=1),
            jnp.sum(jnp.where(picked, student_logits, 0.0), axis=1),
            jnp.sum(jnp.where(picked, teacher_logits, 0.0), axis=1),
            jnp.zeros_like(local_tmax),
        ]
    )
    every = voc_gather(stats, voc_count, 3)
    teacher_max = jnp.max(every[:, 0], axis=0)
    student_max = jnp.max(every[:, 1], axis=0)
    teacher_scale = jnp.exp(every[:, 0] - teacher_max[None, :])
    student_scale = jnp.exp(every[:, 1] - student_max[None, :])
    teacher_sum = jnp.sum(every[:, 2] * teacher_scale, axis=0)
    student_sum = jnp.sum(every[:, 3] * student_scale, axis=0)
    cross_sum = jnp.sum(every[:, 4] * student_scale, axis=0)
    picked_s = jnp.sum(every[:, 5], axis=0)
    picked_t = jnp.sum(every[:, 6], axis=0)
    teacher_norm = teacher_max + jnp.log(teacher_sum)
    student_norm = student_max + jnp.log(student_sum)
    expect = cross_sum / student_sum
    token_loss = (
        expect - student_norm + teacher_norm + (picked_s - student_norm) - (picked_t - teacher_norm)
    )
    student_prob = jnp.exp(student_logits - student_norm[:, None])
    logit_grad = (
        token_weight[:, None]
        * (student_prob * (differ - expect[:, None]) + picked.astype(jnp.float32) - student_prob)
    ).astype(jnp.bfloat16)
    grad_terms = lax.dot_general(
        lax.all_gather(logit_grad, "tok", axis=0, tiled=True),
        student_head,
        (((1,), (1,)), ((), ())),
        preferred_element_type=jnp.float32,
    )
    hidden_grad = lax.psum_scatter(
        grad_terms.astype(jnp.bfloat16), "voc", scatter_dimension=0, tiled=True
    )
    return (token_loss, hidden_grad)


def solution(mesh):
    in_specs = (
        P(("tok", "voc"), None),
        P(("tok", "voc"), None),
        P(("tok", "voc"), None),
        P(None, ("tok", "voc")),
        P(None, ("tok", "voc")),
        P(("tok", "voc"), None),
        P(),
        P("tok", "voc"),
        P("voc", "tok"),
        P("tok", "voc"),
        P("tok"),
        P("tok"),
    )
    out_specs = (P("tok"), P("voc", "tok"))
    return jax.shard_map(
        per_device, mesh=mesh, in_specs=in_specs, out_specs=out_specs, check_vma=False
    )
```

```python
import functools
import jax
import jax.numpy as jnp
from jax import lax
from jax.experimental import pallas as pl
from jax.experimental.pallas import tpu as pltpu
from jax.sharding import PartitionSpec as P

MESH = pl.DeviceIdType.MESH


def route_tables(expert_ids, gate_raw, experts, capacity):
    rows_here, top_k = expert_ids.shape
    flat_ids = expert_ids.reshape(-1)
    one_hot = (flat_ids[:, None] == jnp.arange(experts, dtype=jnp.int32)[None, :]).astype(jnp.int32)
    earlier = jnp.cumsum(one_hot, axis=0, dtype=jnp.int32) - one_hot
    slot_of = jnp.sum(earlier * one_hot, axis=1, dtype=jnp.int32)
    where_to = (flat_ids * capacity + slot_of).reshape(rows_here, top_k)
    columns = jnp.arange(experts * capacity, dtype=jnp.int32)
    matched = where_to[:, :, None] == columns[None, None, :]
    shares = gate_raw / jnp.sum(gate_raw, axis=1, keepdims=True)
    combine_table = jnp.sum(jnp.where(matched, shares[:, :, None], 0.0), axis=1)
    dispatch_table = jnp.transpose(jnp.any(matched, axis=1)).astype(jnp.bfloat16)
    return (dispatch_table, combine_table)


def gather_kernel(n, x_ref, out_ref, send_sem, recv_sem, own_sem):
    t, me = lax.axis_index("tok"), lax.axis_index("voc")
    barrier = pltpu.get_barrier_semaphore()

    @pl.loop(1, n)
    def _(k):
        pl.semaphore_signal(
            barrier, inc=1, device_id=(t, lax.rem(me + k, n)), device_id_type=MESH
        )

    pl.semaphore_wait(barrier, n - 1)

    def copy(k):
        return pltpu.make_async_remote_copy(
            src_ref=x_ref,
            dst_ref=out_ref.at[me],
            send_sem=send_sem.at[k],
            recv_sem=recv_sem.at[k],
            device_id=(t, lax.rem(me + k, n)),
            device_id_type=MESH,
        )

    @pl.loop(1, n)
    def _(k):
        copy(k).start()

    own = pltpu.make_async_copy(x_ref, out_ref.at[me], own_sem)
    own.start()
    own.wait()

    @pl.loop(1, n)
    def _(k):
        pltpu.make_async_remote_copy(
            src_ref=x_ref,
            dst_ref=out_ref.at[lax.rem(me - k + n, n)],
            send_sem=send_sem.at[k],
            recv_sem=recv_sem.at[k],
            device_id=(t, lax.rem(me + k, n)),
            device_id_type=MESH,
        ).wait()


def voc_gather(x, n, collective_id):
    return pl.pallas_call(
        functools.partial(gather_kernel, n),
        out_shape=jax.ShapeDtypeStruct((n,) + x.shape, x.dtype),
        in_specs=[pl.BlockSpec(memory_space=pltpu.VMEM)],
        out_specs=pl.BlockSpec(memory_space=pltpu.VMEM),
        scratch_shapes=[
            pltpu.SemaphoreType.DMA((n,)),
            pltpu.SemaphoreType.DMA((n,)),
            pltpu.SemaphoreType.DMA,
        ],
        compiler_params=pltpu.CompilerParams(collective_id=collective_id, has_side_effects=True),
    )(x)


def grad_kernel(
    g_ref, own_hbm, pair_hbm, out_ref,
    own_w, pair_w, blocks, terms, landed,
    load_sem, ring_send, ring_recv, term_send, term_recv, self_sem,
):
    t, v = lax.axis_index("tok"), lax.axis_index("voc")
    core = lax.rem(t, 2)
    chip = t // 2
    partner = t + 1 - 2 * core
    right, left = lax.rem(t + 2, 8), lax.rem(t + 6, 8)
    half = g_ref.shape[0] // 2
    source_core = lax.rem(v // 2, 2)
    loads = (
        pltpu.make_async_copy(own_hbm, own_w, load_sem.at[0]),
        pltpu.make_async_copy(pair_hbm, pair_w, load_sem.at[1]),
    )
    for load in loads:
        load.start()

    barrier = pltpu.get_barrier_semaphore()
    for side in (right, left):
        pl.semaphore_signal(barrier, inc=1, device_id=(side, v), device_id_type=MESH)

    @pl.loop(0, 16)
    def _(k):
        @pl.when(jnp.logical_or(source_core != core, k != v))
        def _():
            pl.semaphore_signal(
                barrier, inc=1, device_id=(chip * 2 + source_core, k), device_id_type=MESH
            )

    @pl.when(source_core == core)
    def _():
        pl.semaphore_wait(barrier, 17)

    @pl.when(source_core != core)
    def _():
        pl.semaphore_wait(barrier, 18)

    top, low = pl.ds(0, half), pl.ds(half, half)
    plan = (
        (g_ref.at[top], blocks.at[0, top], right),
        (g_ref.at[low], blocks.at[0, low], right),
        (g_ref.at[low], blocks.at[1, low], left),
        (g_ref.at[top], blocks.at[1, top], left),
        (blocks.at[0, top], blocks.at[2, top], right),
        (blocks.at[1, low], blocks.at[2, low], left),
    )
    ring = [
        pltpu.make_async_remote_copy(
            src_ref=source,
            dst_ref=target,
            send_sem=ring_send.at[i],
            recv_sem=ring_recv.at[i],
            device_id=(device, v),
            device_id_type=MESH,
        )
        for i, (source, target, device) in enumerate(plan)
    ]
    for i in (0, 2, 1, 3):
        ring[i].start()
    for load in loads:
        load.wait()

    def term_copy(slot, side, h, piece):
        return pltpu.make_async_remote_copy(
            src_ref=terms.at[slot, side, pl.ds(h * half, half)],
            dst_ref=landed.at[v],
            send_sem=term_send.at[slot * 4 + side * 2 + h],
            recv_sem=term_recv.at[v],
            device_id=(partner if side else t, piece),
            device_id_type=MESH,
        )

    def self_copy(slot, h):
        return pltpu.make_async_copy(
            terms.at[slot, 0, pl.ds(h * half, half)], landed.at[v], self_sem
        )

    pieces = [
        [lax.rem(chip + shift, 4) * 4 + 2 * core + h for h in range(2)] for shift in (0, 3, 1, 2)
    ]

    def multiply(slot, block):
        for side, weight in enumerate((own_w, pair_w)):
            terms[slot, side] = lax.dot_general(
                block[...], weight[...], (((1,), (1,)), ((), ())), preferred_element_type=jnp.float32
            ).astype(jnp.bfloat16)
            for h in range(2):
                piece = pieces[slot][h]
                if side:
                    term_copy(slot, side, h, piece).start()
                else:
                    pl.when(piece != v)(term_copy(slot, side, h, piece).start)
                    pl.when(piece == v)(self_copy(slot, h).start)

    multiply(0, g_ref)
    ring[0].wait_recv()
    ring[4].start()
    ring[2].wait_recv()
    ring[5].start()
    ring[1].wait_recv()
    multiply(1, blocks.at[0])
    ring[3].wait_recv()
    multiply(2, blocks.at[1])
    ring[4].wait_recv()
    ring[5].wait_recv()
    multiply(3, blocks.at[2])

    for slot in range(4):
        for h in range(2):
            piece = pieces[slot][h]
            term_copy(slot, 1, h, piece).wait_send()
            pl.when(piece != v)(term_copy(slot, 0, h, piece).wait_send)
            pl.when(piece == v)(self_copy(slot, h).wait)
    for copy in ring:
        copy.wait_send()

    @pl.loop(0, 16)
    def _(k):
        @pl.when(jnp.logical_or(source_core != core, k != v))
        def _():
            pltpu.make_async_remote_copy(
                src_ref=terms.at[0, 0, top],
                dst_ref=landed.at[k],
                send_sem=term_send.at[0],
                recv_sem=term_recv.at[k],
                device_id=(partner, v),
                device_id_type=MESH,
            ).wait_recv()

    total = landed[0].astype(jnp.float32)
    for k in range(1, 16):
        total += landed[k].astype(jnp.float32)
    out_ref[...] = total.astype(out_ref.dtype)


def grad_reduce(logit_grad, head_own, head_pair, collective_id):
    rows, columns = logit_grad.shape
    width = head_own.shape[0]
    return pl.pallas_call(
        grad_kernel,
        out_shape=jax.ShapeDtypeStruct((rows // 2, width), jnp.bfloat16),
        in_specs=[
            pl.BlockSpec(memory_space=pltpu.VMEM),
            pl.BlockSpec(memory_space=pl.ANY),
            pl.BlockSpec(memory_space=pl.ANY),
        ],
        out_specs=pl.BlockSpec(memory_space=pltpu.VMEM),
        scratch_shapes=[
            pltpu.VMEM((width, columns), jnp.bfloat16),
            pltpu.VMEM((width, columns), jnp.bfloat16),
            pltpu.VMEM((3, rows, columns), jnp.bfloat16),
            pltpu.VMEM((4, 2, rows, width), jnp.bfloat16),
            pltpu.VMEM((16, rows // 2, width), jnp.bfloat16),
            pltpu.SemaphoreType.DMA((2,)),
            pltpu.SemaphoreType.DMA((6,)),
            pltpu.SemaphoreType.DMA((6,)),
            pltpu.SemaphoreType.DMA((16,)),
            pltpu.SemaphoreType.DMA((16,)),
            pltpu.SemaphoreType.DMA,
        ],
        compiler_params=pltpu.CompilerParams(
            collective_id=collective_id, has_side_effects=True, vmem_limit_bytes=56 * 1024 * 1024
        ),
    )(logit_grad, head_own, head_pair)


def per_device(
    tokens_in,
    gate_raw,
    expert_ids,
    w_gate,
    w_up,
    w_down,
    final_gain,
    teacher_head,
    student_hidden,
    student_head,
    sampled_ids,
    token_weight,
):
    tok_count = lax.axis_size("tok")
    voc_count = lax.axis_size("voc")
    experts = tok_count * voc_count // 2
    rows_here, top_k = expert_ids.shape
    model_width = tokens_in.shape[1]
    capacity = max(2, 2 * rows_here * top_k // experts)
    dispatch_table, combine_table = route_tables(expert_ids, gate_raw, experts, capacity)
    dispatched = jnp.dot(dispatch_table, tokens_in, preferred_element_type=jnp.float32).astype(
        jnp.bfloat16
    )
    outgoing = jnp.repeat(dispatched.reshape(experts, capacity, model_width), 2, axis=0)
    student_pair = lax.ppermute(student_head, "tok", [(i, i ^ 1) for i in range(tok_count)])
    student_all = voc_gather(student_hidden, voc_count, 1).reshape(-1, student_hidden.shape[1])
    student_part = jnp.dot(student_all, student_head, preferred_element_type=jnp.float32)
    outgoing, student_part = lax.optimization_barrier((outgoing, student_part))
    student_logits = lax.psum_scatter(student_part, "tok", scatter_dimension=0, tiled=True)
    arrived = lax.all_to_all(outgoing, ("tok", "voc"), split_axis=0, concat_axis=0, tiled=True)
    expert_rows = arrived.reshape(2 * experts * capacity, model_width)
    gate_part = jnp.dot(expert_rows, w_gate, preferred_element_type=jnp.float32)
    up_part = jnp.dot(expert_rows, w_up, preferred_element_type=jnp.float32)
    hidden_units = (jax.nn.silu(gate_part) * up_part).astype(jnp.bfloat16)
    partial_out = (
        jnp.dot(hidden_units, w_down, preferred_element_type=jnp.float32)
        .astype(jnp.bfloat16)
        .reshape(2 * experts, capacity, model_width)
    )
    returned = lax.all_to_all(partial_out, ("tok", "voc"), split_axis=0, concat_axis=0, tiled=True)
    pair_sum = jnp.sum(
        returned.astype(jnp.float32).reshape(experts, 2, capacity, model_width), axis=1
    ).reshape(experts * capacity, model_width)
    expert_mix = jnp.dot(combine_table, pair_sum, precision=lax.Precision.HIGHEST)
    residual_sum = tokens_in.astype(jnp.float32) + expert_mix
    inverse = lax.rsqrt(jnp.mean(residual_sum * residual_sum, axis=1, keepdims=True) + 1e-06)
    normed = (residual_sum * inverse * final_gain[None, :]).astype(jnp.bfloat16)
    tok_rows = voc_gather(normed, voc_count, 2).reshape(-1, model_width)
    teacher_cols = lax.all_to_all(tok_rows, "tok", split_axis=1, concat_axis=0, tiled=True)
    vocab_local = teacher_head.shape[1]
    teacher_part = jnp.dot(teacher_cols, teacher_head, preferred_element_type=jnp.float32)
    teacher_part, student_logits = lax.optimization_barrier(
        (teacher_part.astype(jnp.bfloat16), student_logits)
    )
    teacher_logits = lax.psum_scatter(
        teacher_part, "tok", scatter_dimension=0, tiled=True
    ).astype(jnp.float32)
    differ = student_logits - teacher_logits
    vocab_start = lax.axis_index("voc") * vocab_local
    picked = sampled_ids[:, None] - vocab_start == jnp.arange(vocab_local, dtype=jnp.int32)[None, :]
    local_tmax = jnp.max(teacher_logits, axis=1)
    local_smax = jnp.max(student_logits, axis=1)
    student_exp = jnp.exp(student_logits - local_smax[:, None])
    stats = jnp.stack(
        [
            local_tmax,
            local_smax,
            jnp.sum(jnp.exp(teacher_logits - local_tmax[:, None]), axis=1),
            jnp.sum(student_exp, axis=1),
            jnp.sum(student_exp * differ, axis=1),
            jnp.sum(jnp.where(picked, student_logits, 0.0), axis=1),
            jnp.sum(jnp.where(picked, teacher_logits, 0.0), axis=1),
            jnp.zeros_like(local_tmax),
        ]
    )
    every = voc_gather(stats, voc_count, 3)
    teacher_max = jnp.max(every[:, 0], axis=0)
    student_max = jnp.max(every[:, 1], axis=0)
    teacher_scale = jnp.exp(every[:, 0] - teacher_max[None, :])
    student_scale = jnp.exp(every[:, 1] - student_max[None, :])
    teacher_sum = jnp.sum(every[:, 2] * teacher_scale, axis=0)
    student_sum = jnp.sum(every[:, 3] * student_scale, axis=0)
    cross_sum = jnp.sum(every[:, 4] * student_scale, axis=0)
    picked_s = jnp.sum(every[:, 5], axis=0)
    picked_t = jnp.sum(every[:, 6], axis=0)
    teacher_norm = teacher_max + jnp.log(teacher_sum)
    student_norm = student_max + jnp.log(student_sum)
    expect = cross_sum / student_sum
    token_loss = (
        expect - student_norm + teacher_norm + (picked_s - student_norm) - (picked_t - teacher_norm)
    )
    student_prob = jnp.exp(student_logits - student_norm[:, None])
    logit_grad = (
        token_weight[:, None]
        * (student_prob * (differ - expect[:, None]) + picked.astype(jnp.float32) - student_prob)
    ).astype(jnp.bfloat16)
    hidden_grad = grad_reduce(logit_grad, student_head, student_pair, 4)
    return (token_loss, hidden_grad)


def solution(mesh):
    in_specs = (
        P(("tok", "voc"), None),
        P(("tok", "voc"), None),
        P(("tok", "voc"), None),
        P(None, ("tok", "voc")),
        P(None, ("tok", "voc")),
        P(("tok", "voc"), None),
        P(),
        P("tok", "voc"),
        P("voc", "tok"),
        P("tok", "voc"),
        P("tok"),
        P("tok"),
    )
    out_specs = (P("tok"), P("voc", "tok"))
    return jax.shard_map(
        per_device, mesh=mesh, in_specs=in_specs, out_specs=out_specs, check_vma=False
    )
```

```python
import functools
import jax
import jax.numpy as jnp
from jax import lax
from jax.experimental import pallas as pl
from jax.experimental.pallas import tpu as pltpu
from jax.sharding import PartitionSpec as P

MESH = pl.DeviceIdType.MESH


def exchange_kernel(axis, n, count, source, target, *refs):
    ins, outs = refs[:count], refs[count : 2 * count]
    send_sem, recv_sem, own_sem = refs[2 * count :]
    me = lax.axis_index(axis)

    def device(k):
        peer = lax.rem(me + k, n)
        if axis == "tok":
            return (peer, lax.axis_index("voc"))
        return (lax.axis_index("tok"), peer)

    barrier = pltpu.get_barrier_semaphore()

    @pl.loop(1, n)
    def _(k):
        pl.semaphore_signal(barrier, inc=1, device_id=device(k), device_id_type=MESH)

    pl.semaphore_wait(barrier, n - 1)

    def copy(i, k, sender):
        return pltpu.make_async_remote_copy(
            src_ref=source(ins[i], lax.rem(me + k, n)),
            dst_ref=target(outs[i], sender),
            send_sem=send_sem.at[i, k],
            recv_sem=recv_sem.at[i, k],
            device_id=device(k),
            device_id_type=MESH,
        )

    for i in range(count):

        @pl.loop(1, n)
        def _(k):
            copy(i, k, me).start()

    for i in range(count):
        own = pltpu.make_async_copy(source(ins[i], me), target(outs[i], me), own_sem)
        own.start()
        own.wait()

    for i in range(count):

        @pl.loop(1, n)
        def _(k):
            copy(i, k, lax.rem(me - k + n, n)).wait()


def whole(ref, peer):
    return ref


def at_peer(ref, peer):
    return ref.at[peer]


def at_pair(ref, peer):
    return ref.at[peer // 2]


def at_second(ref, peer):
    return ref.at[:, peer]


def at_core_chip(ref, peer):
    return ref.at[lax.rem(peer, 2) * 4 + peer // 2]


def at_core_features(ref, peer):
    rows = pl.ds(pl.multiple_of(lax.rem(peer, 2) * 32, 32), 32)
    return ref.at[rows, pl.ds(pl.multiple_of((peer // 2) * 1024, 1024), 1024)]


def exchange(arrays, shapes, axis, collective_id, source=whole, target=at_peer):
    n = lax.axis_size(axis)
    count = len(arrays)
    return pl.pallas_call(
        functools.partial(exchange_kernel, axis, n, count, source, target),
        out_shape=[jax.ShapeDtypeStruct(o, x.dtype) for o, x in zip(shapes, arrays)],
        in_specs=[pl.BlockSpec(memory_space=pltpu.VMEM)] * count,
        out_specs=[pl.BlockSpec(memory_space=pltpu.VMEM)] * count,
        scratch_shapes=[
            pltpu.SemaphoreType.DMA((count, n)),
            pltpu.SemaphoreType.DMA((count, n)),
            pltpu.SemaphoreType.DMA,
        ],
        compiler_params=pltpu.CompilerParams(collective_id=collective_id, has_side_effects=True),
    )(*arrays)


def grad_kernel(
    g_ref, own_hbm, pair_hbm, out_ref,
    own_w, pair_w, blocks, terms, landed,
    load_sem, ring_send, ring_recv, term_send, term_recv, self_sem,
):
    t, v = lax.axis_index("tok"), lax.axis_index("voc")
    core = lax.rem(t, 2)
    chip = t // 2
    partner = t + 1 - 2 * core
    right, left = lax.rem(t + 2, 8), lax.rem(t + 6, 8)
    half = g_ref.shape[0] // 2
    source_core = lax.rem(v // 2, 2)
    loads = (
        pltpu.make_async_copy(own_hbm, own_w, load_sem.at[0]),
        pltpu.make_async_copy(pair_hbm, pair_w, load_sem.at[1]),
    )
    for load in loads:
        load.start()

    barrier = pltpu.get_barrier_semaphore()
    for side in (right, left):
        pl.semaphore_signal(barrier, inc=1, device_id=(side, v), device_id_type=MESH)

    @pl.loop(0, 16)
    def _(k):
        @pl.when(jnp.logical_or(source_core != core, k != v))
        def _():
            pl.semaphore_signal(
                barrier, inc=1, device_id=(chip * 2 + source_core, k), device_id_type=MESH
            )

    @pl.when(source_core == core)
    def _():
        pl.semaphore_wait(barrier, 17)

    @pl.when(source_core != core)
    def _():
        pl.semaphore_wait(barrier, 18)

    top, low = pl.ds(0, half), pl.ds(half, half)
    plan = (
        (g_ref.at[top], blocks.at[0, top], right),
        (g_ref.at[low], blocks.at[0, low], right),
        (g_ref.at[low], blocks.at[1, low], left),
        (g_ref.at[top], blocks.at[1, top], left),
        (blocks.at[0, top], blocks.at[2, top], right),
        (blocks.at[1, low], blocks.at[2, low], left),
    )
    ring = [
        pltpu.make_async_remote_copy(
            src_ref=source,
            dst_ref=target,
            send_sem=ring_send.at[i],
            recv_sem=ring_recv.at[i],
            device_id=(device, v),
            device_id_type=MESH,
        )
        for i, (source, target, device) in enumerate(plan)
    ]
    for i in (0, 2, 1, 3):
        ring[i].start()
    for load in loads:
        load.wait()

    def term_copy(slot, side, h, piece):
        return pltpu.make_async_remote_copy(
            src_ref=terms.at[slot, side, pl.ds(h * half, half)],
            dst_ref=landed.at[v],
            send_sem=term_send.at[slot * 4 + side * 2 + h],
            recv_sem=term_recv.at[v],
            device_id=(partner if side else t, piece),
            device_id_type=MESH,
        )

    def self_copy(slot, h):
        return pltpu.make_async_copy(
            terms.at[slot, 0, pl.ds(h * half, half)], landed.at[v], self_sem
        )

    pieces = [
        [lax.rem(chip + shift, 4) * 4 + 2 * core + h for h in range(2)] for shift in (0, 3, 1, 2)
    ]

    def multiply(slot, block):
        for side, weight in enumerate((own_w, pair_w)):
            terms[slot, side] = lax.dot_general(
                block[...], weight[...], (((1,), (1,)), ((), ())), preferred_element_type=jnp.float32
            ).astype(jnp.bfloat16)
            for h in range(2):
                piece = pieces[slot][h]
                if side:
                    term_copy(slot, side, h, piece).start()
                else:
                    pl.when(piece != v)(term_copy(slot, side, h, piece).start)
                    pl.when(piece == v)(self_copy(slot, h).start)

    multiply(0, g_ref)
    ring[0].wait_recv()
    ring[4].start()
    ring[2].wait_recv()
    ring[5].start()
    ring[1].wait_recv()
    multiply(1, blocks.at[0])
    ring[3].wait_recv()
    multiply(2, blocks.at[1])
    ring[4].wait_recv()
    ring[5].wait_recv()
    multiply(3, blocks.at[2])

    for slot in range(4):
        for h in range(2):
            piece = pieces[slot][h]
            term_copy(slot, 1, h, piece).wait_send()
            pl.when(piece != v)(term_copy(slot, 0, h, piece).wait_send)
            pl.when(piece == v)(self_copy(slot, h).wait)
    for copy in ring:
        copy.wait_send()

    @pl.loop(0, 16)
    def _(k):
        @pl.when(jnp.logical_or(source_core != core, k != v))
        def _():
            pltpu.make_async_remote_copy(
                src_ref=terms.at[0, 0, top],
                dst_ref=landed.at[k],
                send_sem=term_send.at[0],
                recv_sem=term_recv.at[k],
                device_id=(partner, v),
                device_id_type=MESH,
            ).wait_recv()

    total = landed[0].astype(jnp.float32)
    for k in range(1, 16):
        total += landed[k].astype(jnp.float32)
    out_ref[...] = total.astype(out_ref.dtype)


def grad_reduce(logit_grad, head_own, head_pair, collective_id):
    rows, columns = logit_grad.shape
    width = head_own.shape[0]
    return pl.pallas_call(
        grad_kernel,
        out_shape=jax.ShapeDtypeStruct((rows // 2, width), jnp.bfloat16),
        in_specs=[
            pl.BlockSpec(memory_space=pltpu.VMEM),
            pl.BlockSpec(memory_space=pl.ANY),
            pl.BlockSpec(memory_space=pl.ANY),
        ],
        out_specs=pl.BlockSpec(memory_space=pltpu.VMEM),
        scratch_shapes=[
            pltpu.VMEM((width, columns), jnp.bfloat16),
            pltpu.VMEM((width, columns), jnp.bfloat16),
            pltpu.VMEM((3, rows, columns), jnp.bfloat16),
            pltpu.VMEM((4, 2, rows, width), jnp.bfloat16),
            pltpu.VMEM((16, rows // 2, width), jnp.bfloat16),
            pltpu.SemaphoreType.DMA((2,)),
            pltpu.SemaphoreType.DMA((6,)),
            pltpu.SemaphoreType.DMA((6,)),
            pltpu.SemaphoreType.DMA((16,)),
            pltpu.SemaphoreType.DMA((16,)),
            pltpu.SemaphoreType.DMA,
        ],
        compiler_params=pltpu.CompilerParams(
            collective_id=collective_id, has_side_effects=True, vmem_limit_bytes=56 * 1024 * 1024
        ),
    )(logit_grad, head_own, head_pair)


def head_kernel(
    rows_ref, squares_ref, own_hbm, pair_hbm, out_ref,
    own_w, pair_w, far, kept, relay, sent, final, squares,
    load_sem, ring_send, ring_recv, square_send, square_recv,
):
    t, v = lax.axis_index("tok"), lax.axis_index("voc")
    core = lax.rem(t, 2)
    chip = t // 2
    right, left, across = lax.rem(t + 2, 8), lax.rem(t + 6, 8), lax.rem(t + 4, 8)
    half = rows_ref.shape[1] // 2
    width = own_w.shape[0]
    features = rows_ref.shape[2] * 4
    loads = (
        pltpu.make_async_copy(own_hbm, own_w, load_sem.at[0]),
        pltpu.make_async_copy(pair_hbm, pair_w, load_sem.at[1]),
    )
    for load in loads:
        load.start()
    barrier = pltpu.get_barrier_semaphore()
    for side in (right, left, across):
        pl.semaphore_signal(barrier, inc=1, device_id=(side, v), device_id_type=MESH)
    pl.semaphore_wait(barrier, 3)

    chips = [lax.rem(chip + shift, 4) for shift in range(4)]
    square_copies = [
        pltpu.make_async_remote_copy(
            src_ref=squares_ref.at[chips[shift]],
            dst_ref=squares.at[shift - 1],
            send_sem=square_send.at[shift - 1],
            recv_sem=square_recv.at[shift - 1],
            device_id=(device, v),
            device_id_type=MESH,
        )
        for shift, device in ((1, right), (2, across), (3, left))
    ]
    top, low = pl.ds(0, half), pl.ds(half, half)
    plan = (
        (far.at[top], relay.at[0], right),
        (far.at[low], relay.at[1], left),
        (sent.at[0, low], final.at[0, low], right),
        (sent.at[1, top], final.at[1, top], left),
        (sent.at[0, top], final.at[0, top], right),
        (sent.at[1, low], final.at[1, low], left),
    )
    ring = [
        pltpu.make_async_remote_copy(
            src_ref=source,
            dst_ref=target,
            send_sem=ring_send.at[i],
            recv_sem=ring_recv.at[i],
            device_id=(device, v),
            device_id_type=MESH,
        )
        for i, (source, target, device) in enumerate(plan)
    ]
    own_columns = pl.ds(pl.multiple_of(core * width, width), width)
    pair_columns = pl.ds(pl.multiple_of((1 - core) * width, width), width)
    step = 256
    steps = own_w.shape[1] // step

    def multiply(shift, store):
        own_rows = rows_ref[chips[shift], :, own_columns]
        pair_rows = rows_ref[chips[shift], :, pair_columns]

        @pl.loop(0, steps)
        def _(j):
            columns = pl.ds(pl.multiple_of(j * step, step), step)
            store(
                columns,
                jnp.dot(own_rows, own_w[:, columns], preferred_element_type=jnp.float32)
                + jnp.dot(pair_rows, pair_w[:, columns], preferred_element_type=jnp.float32),
            )

    def store_far(columns, value):
        far[:, columns] = value.astype(jnp.bfloat16)

    def store_right(columns, value):
        kept[0, :, columns] = value[:half]
        sent[0, low, columns] = value[half:].astype(jnp.bfloat16)

    def store_left(columns, value):
        kept[1, :, columns] = value[half:]
        sent[1, top, columns] = value[:half].astype(jnp.bfloat16)

    def store_own(columns, value):
        out_ref[:, columns] = value

    for load in loads:
        load.wait()
    multiply(2, store_far)
    ring[0].start()
    ring[1].start()
    multiply(1, store_right)
    ring[2].start()
    multiply(3, store_left)
    ring[3].start()
    for copy in square_copies:
        copy.start()
    multiply(0, store_own)
    for i, rows in ((0, top), (1, low)):
        ring[i].wait_recv()

        @pl.loop(0, steps)
        def _(j):
            columns = pl.ds(pl.multiple_of(j * step, step), step)
            sent[i, rows, columns] = (
                kept[i, :, columns] + relay[i, :, columns].astype(jnp.float32)
            ).astype(jnp.bfloat16)

        ring[4 + i].start()
    total = squares_ref[chip]
    for i, copy in enumerate(square_copies):
        copy.wait_recv()
        total += squares[i]
    inverse = lax.rsqrt(total[:, :1] / features + 1e-06)
    for i in range(2, 6):
        ring[i].wait_recv()

    @pl.loop(0, steps)
    def _(j):
        columns = pl.ds(pl.multiple_of(j * step, step), step)
        out_ref[:, columns] = (
            out_ref[:, columns]
            + final[0, :, columns].astype(jnp.float32)
            + final[1, :, columns].astype(jnp.float32)
        ) * inverse

    for copy in square_copies:
        copy.wait_send()
    for copy in ring:
        copy.wait_send()


def head_reduce(rows, squares, head_own, head_pair, collective_id):
    chips, count, _ = rows.shape
    width, columns = head_own.shape
    vmem = pl.BlockSpec(memory_space=pltpu.VMEM)
    hbm = pl.BlockSpec(memory_space=pl.ANY)
    return pl.pallas_call(
        head_kernel,
        out_shape=jax.ShapeDtypeStruct((count, columns), jnp.float32),
        in_specs=[vmem, vmem, hbm, hbm],
        out_specs=vmem,
        scratch_shapes=[
            pltpu.VMEM((width, columns), jnp.bfloat16),
            pltpu.VMEM((width, columns), jnp.bfloat16),
            pltpu.VMEM((count, columns), jnp.bfloat16),
            pltpu.VMEM((2, count // 2, columns), jnp.float32),
            pltpu.VMEM((2, count // 2, columns), jnp.bfloat16),
            pltpu.VMEM((2, count, columns), jnp.bfloat16),
            pltpu.VMEM((2, count, columns), jnp.bfloat16),
            pltpu.VMEM((3, count, 128), jnp.float32),
            pltpu.SemaphoreType.DMA((2,)),
            pltpu.SemaphoreType.DMA((6,)),
            pltpu.SemaphoreType.DMA((6,)),
            pltpu.SemaphoreType.DMA((3,)),
            pltpu.SemaphoreType.DMA((3,)),
        ],
        compiler_params=pltpu.CompilerParams(
            collective_id=collective_id, has_side_effects=True, vmem_limit_bytes=56 * 1024 * 1024
        ),
    )(rows, squares, head_own, head_pair)


def per_device(
    tokens_in,
    gate_raw,
    expert_ids,
    w_gate,
    w_up,
    w_down,
    final_gain,
    teacher_head,
    student_hidden,
    student_head,
    sampled_ids,
    token_weight,
):
    tok_count = lax.axis_size("tok")
    voc_count = lax.axis_size("voc")
    rows_here, top_k = expert_ids.shape
    model_width = tokens_in.shape[1]
    part_width = model_width // tok_count
    student_pair = lax.ppermute(student_head, "tok", [(i, i ^ 1) for i in range(tok_count)])
    teacher_pair = lax.ppermute(teacher_head, "tok", [(i, i ^ 1) for i in range(tok_count)])
    student_all = lax.all_gather(student_hidden, "voc", axis=0, tiled=True)
    student_part = jnp.dot(student_all, student_head, preferred_element_type=jnp.float32)
    ids_shares = jnp.concatenate(
        [expert_ids.astype(jnp.float32), gate_raw, jnp.zeros((rows_here, 128 - 2 * top_k), jnp.float32)],
        axis=1,
    )
    rows_all = tok_count * rows_here
    tokens_all, table = exchange(
        [tokens_in, ids_shares],
        [(tok_count, rows_here, model_width), (tok_count, rows_here, 128)],
        "tok",
        2,
        target=at_core_chip,
    )
    tokens_all = tokens_all.reshape(rows_all, model_width)
    table = table.reshape(rows_all, 128)
    slots = 2
    here = voc_count // 2
    column = jnp.arange(here * tok_count * slots, dtype=jnp.int32)
    column_expert = column // (tok_count * slots) + lax.axis_index("tok") * here
    column_block = column // slots % tok_count
    column_slot = column % slots
    row = jnp.arange(rows_all, dtype=jnp.int32)
    gates = table[:, top_k : 2 * top_k]
    shares = gates / jnp.sum(gates, axis=1, keepdims=True)
    named = [
        table[:, k : k + 1] == column_expert.astype(jnp.float32)[None, :] for k in range(top_k)
    ]
    present = functools.reduce(jnp.logical_or, named)
    share_of = sum(jnp.where(named[k], shares[:, k : k + 1], 0.0) for k in range(top_k))
    before = (row[:, None] // rows_here == row[None, :] // rows_here) & (row[None, :] < row[:, None])
    earlier = jnp.dot(
        before.astype(jnp.bfloat16), present.astype(jnp.bfloat16), preferred_element_type=jnp.float32
    )
    matched = (
        present
        & (earlier == column_slot.astype(jnp.float32)[None, :])
        & (row[:, None] // rows_here == column_block[None, :])
    )
    combine_table = jnp.where(matched, share_of, 0.0)
    dispatched = lax.dot_general(
        matched.astype(jnp.bfloat16),
        tokens_all,
        (((0,), (0,)), ((), ())),
        preferred_element_type=jnp.float32,
    ).astype(jnp.bfloat16)
    group = tok_count * slots
    (arrived,) = exchange(
        [dispatched.reshape(here, group, model_width)],
        [(voc_count, group, model_width)],
        "voc",
        3,
        source=at_pair,
    )
    arrived, student_part = lax.optimization_barrier((arrived, student_part))
    student_logits = lax.psum_scatter(student_part, "tok", scatter_dimension=0, tiled=True)
    expert_rows = arrived.reshape(voc_count * group, model_width)
    gate_part = jnp.dot(expert_rows, w_gate, preferred_element_type=jnp.float32)
    up_part = jnp.dot(expert_rows, w_up, preferred_element_type=jnp.float32)
    hidden_units = (jax.nn.silu(gate_part) * up_part).astype(jnp.bfloat16)
    partial_out = jnp.dot(hidden_units, w_down, preferred_element_type=jnp.float32).astype(
        jnp.bfloat16
    )
    (returned,) = exchange(
        [partial_out.reshape(voc_count, group, model_width)],
        [(voc_count, group, model_width)],
        "voc",
        5,
        source=at_peer,
    )
    pair_sum = jnp.sum(
        returned.astype(jnp.float32).reshape(here, 2, group, model_width), axis=1
    ).reshape(here * group, model_width)
    mix_part = jnp.dot(combine_table, pair_sum, precision=lax.Precision.HIGHEST)
    core_rows, chip_width = rows_all // 2, 2 * part_width
    (mix_parts,) = exchange(
        [mix_part], [(tok_count, core_rows, chip_width)], "tok", 6, source=at_core_features
    )
    tok_index = lax.axis_index("tok")
    feature_start = (tok_index // 2) * chip_width
    tokens_part = lax.dynamic_slice(
        tokens_all, ((tok_index % 2) * core_rows, feature_start), (core_rows, chip_width)
    )
    residual_sum = tokens_part.astype(jnp.float32) + jnp.sum(mix_parts, axis=0)
    squares = jnp.sum(residual_sum * residual_sum, axis=1, keepdims=True)
    gain_part = lax.dynamic_slice_in_dim(final_gain, feature_start, chip_width, 0)
    scaled = (residual_sum * gain_part[None, :]).astype(jnp.bfloat16)
    chips = tok_count // 2
    teacher_rows, squares_rows = exchange(
        [
            scaled.reshape(chips, rows_here, chip_width),
            jnp.broadcast_to(squares, (core_rows, 128)).reshape(chips, rows_here, 128),
        ],
        [
            (chips, voc_count, rows_here, chip_width),
            (chips, voc_count, rows_here, 128),
        ],
        "voc",
        8,
        target=at_second,
    )
    vocab_local = teacher_head.shape[1]
    teacher_logits = head_reduce(
        teacher_rows.reshape(chips, voc_count * rows_here, chip_width),
        squares_rows.reshape(chips, voc_count * rows_here, 128),
        teacher_head,
        teacher_pair,
        10,
    )
    differ = student_logits - teacher_logits
    vocab_start = lax.axis_index("voc") * vocab_local
    picked = sampled_ids[:, None] - vocab_start == jnp.arange(vocab_local, dtype=jnp.int32)[None, :]
    local_tmax = jnp.max(teacher_logits, axis=1)
    local_smax = jnp.max(student_logits, axis=1)
    student_exp = jnp.exp(student_logits - local_smax[:, None])
    stats = jnp.stack(
        [
            local_tmax,
            local_smax,
            jnp.sum(jnp.exp(teacher_logits - local_tmax[:, None]), axis=1),
            jnp.sum(student_exp, axis=1),
            jnp.sum(student_exp * differ, axis=1),
            jnp.sum(jnp.where(picked, student_logits, 0.0), axis=1),
            jnp.sum(jnp.where(picked, teacher_logits, 0.0), axis=1),
            jnp.zeros_like(local_tmax),
        ]
    )
    (every,) = exchange([stats], [(voc_count,) + stats.shape], "voc", 9)
    teacher_max = jnp.max(every[:, 0], axis=0)
    student_max = jnp.max(every[:, 1], axis=0)
    teacher_scale = jnp.exp(every[:, 0] - teacher_max[None, :])
    student_scale = jnp.exp(every[:, 1] - student_max[None, :])
    teacher_sum = jnp.sum(every[:, 2] * teacher_scale, axis=0)
    student_sum = jnp.sum(every[:, 3] * student_scale, axis=0)
    cross_sum = jnp.sum(every[:, 4] * student_scale, axis=0)
    picked_s = jnp.sum(every[:, 5], axis=0)
    picked_t = jnp.sum(every[:, 6], axis=0)
    teacher_norm = teacher_max + jnp.log(teacher_sum)
    student_norm = student_max + jnp.log(student_sum)
    expect = cross_sum / student_sum
    token_loss = (
        expect - student_norm + teacher_norm + (picked_s - student_norm) - (picked_t - teacher_norm)
    )
    student_prob = jnp.exp(student_logits - student_norm[:, None])
    logit_grad = (
        token_weight[:, None]
        * (student_prob * (differ - expect[:, None]) + picked.astype(jnp.float32) - student_prob)
    ).astype(jnp.bfloat16)
    hidden_grad = grad_reduce(logit_grad, student_head, student_pair, 4)
    return (token_loss, hidden_grad)


def solution(mesh):
    in_specs = (
        P(("tok", "voc"), None),
        P(("tok", "voc"), None),
        P(("tok", "voc"), None),
        P(None, ("tok", "voc")),
        P(None, ("tok", "voc")),
        P(("tok", "voc"), None),
        P(),
        P("tok", "voc"),
        P("voc", "tok"),
        P("tok", "voc"),
        P("tok"),
        P("tok"),
    )
    out_specs = (P("tok"), P("voc", "tok"))
    return jax.shard_map(
        per_device, mesh=mesh, in_specs=in_specs, out_specs=out_specs, check_vma=False
    )
```

```python
import functools
import jax
import jax.numpy as jnp
from jax import lax
from jax.experimental import pallas as pl
from jax.experimental.pallas import tpu as pltpu
from jax.sharding import PartitionSpec as P

MESH = pl.DeviceIdType.MESH


def device_on(axis, index):
    if axis == "tok":
        return (index, lax.axis_index("voc"))
    return (lax.axis_index("tok"), index)


def exchange_kernel(axes, sizes, source, targets, *refs):
    count = len(axes)
    ins, outs = refs[:count], refs[count : 2 * count]
    send_sem, recv_sem, own_sem = refs[2 * count :]
    barrier = pltpu.get_barrier_semaphore()
    for axis in sorted(set(axes)):
        n = sizes[axis]

        @pl.loop(1, n)
        def _(k):
            peer = lax.rem(lax.axis_index(axis) + k, n)
            pl.semaphore_signal(barrier, inc=1, device_id=device_on(axis, peer), device_id_type=MESH)

    pl.semaphore_wait(barrier, sum(sizes[axis] - 1 for axis in set(axes)))

    def copy(i, k, back):
        me, n = lax.axis_index(axes[i]), sizes[axes[i]]
        peer = lax.rem(me + k, n)
        return pltpu.make_async_remote_copy(
            src_ref=source(ins[i], peer),
            dst_ref=targets[i](outs[i], lax.rem(me - k + n, n) if back else me),
            send_sem=send_sem.at[i, k],
            recv_sem=recv_sem.at[i, k],
            device_id=device_on(axes[i], peer),
            device_id_type=MESH,
        )

    for i in range(count):

        @pl.loop(1, sizes[axes[i]])
        def _(k):
            copy(i, k, False).start()

    for i in range(count):
        me = lax.axis_index(axes[i])
        own = pltpu.make_async_copy(source(ins[i], me), targets[i](outs[i], me), own_sem)
        own.start()
        own.wait()

    for i in range(count):

        @pl.loop(1, sizes[axes[i]])
        def _(k):
            copy(i, k, True).wait()


def whole(ref, peer):
    return ref


def at_peer(ref, peer):
    return ref.at[peer]


def at_pair(ref, peer):
    return ref.at[peer // 2]


def at_second(ref, peer):
    return ref.at[:, peer]


def at_core_chip(ref, peer):
    return ref.at[lax.rem(peer, 2) * 4 + peer // 2]


def at_core_features(ref, peer):
    rows = pl.ds(pl.multiple_of(lax.rem(peer, 2) * 32, 32), 32)
    return ref.at[rows, pl.ds(pl.multiple_of((peer // 2) * 1024, 1024), 1024)]


def exchange(arrays, shapes, axes, collective_id, source=whole, targets=None):
    count = len(arrays)
    sizes = {axis: lax.axis_size(axis) for axis in axes}
    return pl.pallas_call(
        functools.partial(
            exchange_kernel, axes, sizes, source, targets or (at_peer,) * count
        ),
        out_shape=[jax.ShapeDtypeStruct(o, x.dtype) for o, x in zip(shapes, arrays)],
        in_specs=[pl.BlockSpec(memory_space=pltpu.VMEM)] * count,
        out_specs=[pl.BlockSpec(memory_space=pltpu.VMEM)] * count,
        scratch_shapes=[
            pltpu.SemaphoreType.DMA((count, max(sizes.values()))),
            pltpu.SemaphoreType.DMA((count, max(sizes.values()))),
            pltpu.SemaphoreType.DMA,
        ],
        compiler_params=pltpu.CompilerParams(collective_id=collective_id, has_side_effects=True),
    )(*arrays)


OFFSETS = (
    (0, 1), (1, 0), (0, 3), (3, 0), (1, 1), (3, 3), (1, 3),
    (3, 1), (2, 0), (0, 2), (1, 2), (2, 1), (3, 2), (2, 3), (2, 2),
)


def expert_kernel(
    x_ref, gate_hbm, up_hbm, down_hbm, out_ref,
    gate_w, up_w, down_w, rows, results,
    load_sem, rows_send, rows_recv, back_send, back_recv, own_sem,
):
    v = lax.axis_index("voc")
    y, z = v // 4, lax.rem(v, 4)
    loads = [
        pltpu.make_async_copy(source, target, load_sem.at[i])
        for i, (source, target) in enumerate(
            ((gate_hbm, gate_w), (up_hbm, up_w), (down_hbm, down_w))
        )
    ]
    for load in loads:
        load.start()

    def ahead(i):
        dy, dz = OFFSETS[i - 1]
        return lax.rem(y + dy, 4) * 4 + lax.rem(z + dz, 4)

    def behind(i):
        dy, dz = OFFSETS[i - 1]
        return lax.rem(y + 4 - dy, 4) * 4 + lax.rem(z + 4 - dz, 4)

    barrier = pltpu.get_barrier_semaphore()
    for i in range(1, 16):
        pl.semaphore_signal(
            barrier, inc=1, device_id=device_on("voc", ahead(i)), device_id_type=MESH
        )
    pl.semaphore_wait(barrier, 15)

    def row_copy(i):
        return pltpu.make_async_remote_copy(
            src_ref=x_ref.at[ahead(i) // 2],
            dst_ref=rows.at[i],
            send_sem=rows_send.at[i],
            recv_sem=rows_recv.at[i],
            device_id=device_on("voc", ahead(i)),
            device_id_type=MESH,
        )

    def back_copy(i, place):
        return pltpu.make_async_remote_copy(
            src_ref=results.at[i],
            dst_ref=out_ref.at[place],
            send_sem=back_send.at[i],
            recv_sem=back_recv.at[i],
            device_id=device_on("voc", behind(i)),
            device_id_type=MESH,
        )

    for i in range(1, 16):
        row_copy(i).start()
    own = pltpu.make_async_copy(x_ref.at[v // 2], rows.at[0], own_sem.at[0])
    own.start()
    for load in loads:
        load.wait()
    own.wait()
    group, width = rows.shape[1:]
    step = 512
    own_back = pltpu.make_async_copy(results.at[0], out_ref.at[v], own_sem.at[1])
    for first in (0, 8):
        for i in range(max(first, 1), first + 8):
            row_copy(i).wait_recv()
        batch = rows[pl.ds(first, 8)].reshape(8 * group, width)
        gate = jnp.dot(batch, gate_w[...], preferred_element_type=jnp.float32)
        up = jnp.dot(batch, up_w[...], preferred_element_type=jnp.float32)
        units = (gate * jax.nn.sigmoid(gate) * up).astype(jnp.bfloat16)

        @pl.loop(0, width // step)
        def _(j):
            columns = pl.ds(pl.multiple_of(j * step, step), step)
            part = jnp.dot(units, down_w[:, columns], preferred_element_type=jnp.float32)
            results[pl.ds(first, 8), :, columns] = part.astype(jnp.bfloat16).reshape(8, group, step)

        for i in range(max(first, 1), first + 8):
            back_copy(i, v).start()
        if first == 0:
            own_back.start()
    own_back.wait()
    for i in range(1, 16):
        row_copy(i).wait_send()
        back_copy(i, ahead(i)).wait()


def expert_layer(x, w_gate, w_up, w_down, collective_id):
    _, group, width = x.shape
    vmem = pl.BlockSpec(memory_space=pltpu.VMEM)
    hbm = pl.BlockSpec(memory_space=pl.ANY)
    return pl.pallas_call(
        expert_kernel,
        out_shape=jax.ShapeDtypeStruct((16, group, width), jnp.bfloat16),
        in_specs=[vmem, hbm, hbm, hbm],
        out_specs=vmem,
        scratch_shapes=[
            pltpu.VMEM(w_gate.shape, jnp.bfloat16),
            pltpu.VMEM(w_up.shape, jnp.bfloat16),
            pltpu.VMEM(w_down.shape, jnp.bfloat16),
            pltpu.VMEM((16, group, width), jnp.bfloat16),
            pltpu.VMEM((16, group, width), jnp.bfloat16),
            pltpu.SemaphoreType.DMA((3,)),
            pltpu.SemaphoreType.DMA((16,)),
            pltpu.SemaphoreType.DMA((16,)),
            pltpu.SemaphoreType.DMA((16,)),
            pltpu.SemaphoreType.DMA((16,)),
            pltpu.SemaphoreType.DMA((2,)),
        ],
        compiler_params=pltpu.CompilerParams(
            collective_id=collective_id, has_side_effects=True, vmem_limit_bytes=56 * 1024 * 1024
        ),
    )(x, w_gate, w_up, w_down)


def grad_kernel(
    g_ref, own_hbm, pair_hbm, out_ref,
    own_w, pair_w, blocks, terms, landed,
    load_sem, ring_send, ring_recv, term_send, term_recv, self_sem,
):
    t, v = lax.axis_index("tok"), lax.axis_index("voc")
    core = lax.rem(t, 2)
    chip = t // 2
    partner = t + 1 - 2 * core
    right, left = lax.rem(t + 2, 8), lax.rem(t + 6, 8)
    half = g_ref.shape[0] // 2
    source_core = lax.rem(v // 2, 2)
    loads = (
        pltpu.make_async_copy(own_hbm, own_w, load_sem.at[0]),
        pltpu.make_async_copy(pair_hbm, pair_w, load_sem.at[1]),
    )
    for load in loads:
        load.start()

    barrier = pltpu.get_barrier_semaphore()
    for side in (right, left):
        pl.semaphore_signal(barrier, inc=1, device_id=(side, v), device_id_type=MESH)

    @pl.loop(0, 16)
    def _(k):
        @pl.when(jnp.logical_or(source_core != core, k != v))
        def _():
            pl.semaphore_signal(
                barrier, inc=1, device_id=(chip * 2 + source_core, k), device_id_type=MESH
            )

    @pl.when(source_core == core)
    def _():
        pl.semaphore_wait(barrier, 17)

    @pl.when(source_core != core)
    def _():
        pl.semaphore_wait(barrier, 18)

    top, low = pl.ds(0, half), pl.ds(half, half)
    plan = (
        (g_ref.at[top], blocks.at[0, top], right),
        (g_ref.at[low], blocks.at[0, low], right),
        (g_ref.at[low], blocks.at[1, low], left),
        (g_ref.at[top], blocks.at[1, top], left),
        (blocks.at[0, top], blocks.at[2, top], right),
        (blocks.at[1, low], blocks.at[2, low], left),
    )
    ring = [
        pltpu.make_async_remote_copy(
            src_ref=source,
            dst_ref=target,
            send_sem=ring_send.at[i],
            recv_sem=ring_recv.at[i],
            device_id=(device, v),
            device_id_type=MESH,
        )
        for i, (source, target, device) in enumerate(plan)
    ]
    for i in (0, 2, 1, 3):
        ring[i].start()
    for load in loads:
        load.wait()

    def term_copy(slot, side, h, piece):
        return pltpu.make_async_remote_copy(
            src_ref=terms.at[slot, side, pl.ds(h * half, half)],
            dst_ref=landed.at[v],
            send_sem=term_send.at[slot * 4 + side * 2 + h],
            recv_sem=term_recv.at[v],
            device_id=(partner if side else t, piece),
            device_id_type=MESH,
        )

    def self_copy(slot, h):
        return pltpu.make_async_copy(
            terms.at[slot, 0, pl.ds(h * half, half)], landed.at[v], self_sem
        )

    pieces = [
        [lax.rem(chip + shift, 4) * 4 + 2 * core + h for h in range(2)] for shift in (0, 3, 1, 2)
    ]

    def multiply(slot, block):
        for side, weight in enumerate((own_w, pair_w)):
            terms[slot, side] = lax.dot_general(
                block[...], weight[...], (((1,), (1,)), ((), ())), preferred_element_type=jnp.float32
            ).astype(jnp.bfloat16)
            for h in range(2):
                piece = pieces[slot][h]
                if side:
                    term_copy(slot, side, h, piece).start()
                else:
                    pl.when(piece != v)(term_copy(slot, side, h, piece).start)
                    pl.when(piece == v)(self_copy(slot, h).start)

    multiply(0, g_ref)
    ring[0].wait_recv()
    ring[4].start()
    ring[2].wait_recv()
    ring[5].start()
    ring[1].wait_recv()
    multiply(1, blocks.at[0])
    ring[3].wait_recv()
    multiply(2, blocks.at[1])
    ring[4].wait_recv()
    ring[5].wait_recv()
    multiply(3, blocks.at[2])

    for slot in range(4):
        for h in range(2):
            piece = pieces[slot][h]
            term_copy(slot, 1, h, piece).wait_send()
            pl.when(piece != v)(term_copy(slot, 0, h, piece).wait_send)
            pl.when(piece == v)(self_copy(slot, h).wait)
    for copy in ring:
        copy.wait_send()

    @pl.loop(0, 16)
    def _(k):
        @pl.when(jnp.logical_or(source_core != core, k != v))
        def _():
            pltpu.make_async_remote_copy(
                src_ref=terms.at[0, 0, top],
                dst_ref=landed.at[k],
                send_sem=term_send.at[0],
                recv_sem=term_recv.at[k],
                device_id=(partner, v),
                device_id_type=MESH,
            ).wait_recv()

    total = landed[0].astype(jnp.float32)
    for k in range(1, 16):
        total += landed[k].astype(jnp.float32)
    out_ref[...] = total.astype(out_ref.dtype)


def grad_reduce(logit_grad, head_own, head_pair, collective_id):
    rows, columns = logit_grad.shape
    width = head_own.shape[0]
    return pl.pallas_call(
        grad_kernel,
        out_shape=jax.ShapeDtypeStruct((rows // 2, width), jnp.bfloat16),
        in_specs=[
            pl.BlockSpec(memory_space=pltpu.VMEM),
            pl.BlockSpec(memory_space=pl.ANY),
            pl.BlockSpec(memory_space=pl.ANY),
        ],
        out_specs=pl.BlockSpec(memory_space=pltpu.VMEM),
        scratch_shapes=[
            pltpu.VMEM((width, columns), jnp.bfloat16),
            pltpu.VMEM((width, columns), jnp.bfloat16),
            pltpu.VMEM((3, rows, columns), jnp.bfloat16),
            pltpu.VMEM((4, 2, rows, width), jnp.bfloat16),
            pltpu.VMEM((16, rows // 2, width), jnp.bfloat16),
            pltpu.SemaphoreType.DMA((2,)),
            pltpu.SemaphoreType.DMA((6,)),
            pltpu.SemaphoreType.DMA((6,)),
            pltpu.SemaphoreType.DMA((16,)),
            pltpu.SemaphoreType.DMA((16,)),
            pltpu.SemaphoreType.DMA,
        ],
        compiler_params=pltpu.CompilerParams(
            collective_id=collective_id, has_side_effects=True, vmem_limit_bytes=56 * 1024 * 1024
        ),
    )(logit_grad, head_own, head_pair)


def head_kernel(
    rows_ref, squares_ref, own_hbm, pair_hbm, out_ref,
    own_w, pair_w, far, kept, relay, sent, final, squares,
    load_sem, ring_send, ring_recv, square_send, square_recv,
):
    t, v = lax.axis_index("tok"), lax.axis_index("voc")
    core = lax.rem(t, 2)
    chip = t // 2
    right, left, across = lax.rem(t + 2, 8), lax.rem(t + 6, 8), lax.rem(t + 4, 8)
    half = rows_ref.shape[1] // 2
    width = own_w.shape[0]
    features = rows_ref.shape[2] * 4
    loads = (
        pltpu.make_async_copy(own_hbm, own_w, load_sem.at[0]),
        pltpu.make_async_copy(pair_hbm, pair_w, load_sem.at[1]),
    )
    for load in loads:
        load.start()
    barrier = pltpu.get_barrier_semaphore()
    for side in (right, left, across):
        pl.semaphore_signal(barrier, inc=1, device_id=(side, v), device_id_type=MESH)
    pl.semaphore_wait(barrier, 3)

    chips = [lax.rem(chip + shift, 4) for shift in range(4)]
    square_copies = [
        pltpu.make_async_remote_copy(
            src_ref=squares_ref.at[chips[shift]],
            dst_ref=squares.at[shift - 1],
            send_sem=square_send.at[shift - 1],
            recv_sem=square_recv.at[shift - 1],
            device_id=(device, v),
            device_id_type=MESH,
        )
        for shift, device in ((1, right), (2, across), (3, left))
    ]
    top, low = pl.ds(0, half), pl.ds(half, half)
    plan = (
        (far.at[top], relay.at[0], right),
        (far.at[low], relay.at[1], left),
        (sent.at[0, low], final.at[0, low], right),
        (sent.at[1, top], final.at[1, top], left),
        (sent.at[0, top], final.at[0, top], right),
        (sent.at[1, low], final.at[1, low], left),
    )
    ring = [
        pltpu.make_async_remote_copy(
            src_ref=source,
            dst_ref=target,
            send_sem=ring_send.at[i],
            recv_sem=ring_recv.at[i],
            device_id=(device, v),
            device_id_type=MESH,
        )
        for i, (source, target, device) in enumerate(plan)
    ]
    own_columns = pl.ds(pl.multiple_of(core * width, width), width)
    pair_columns = pl.ds(pl.multiple_of((1 - core) * width, width), width)
    step = 256
    steps = own_w.shape[1] // step

    def multiply(shift, store):
        own_rows = rows_ref[chips[shift], :, own_columns]
        pair_rows = rows_ref[chips[shift], :, pair_columns]

        @pl.loop(0, steps)
        def _(j):
            columns = pl.ds(pl.multiple_of(j * step, step), step)
            store(
                columns,
                jnp.dot(own_rows, own_w[:, columns], preferred_element_type=jnp.float32)
                + jnp.dot(pair_rows, pair_w[:, columns], preferred_element_type=jnp.float32),
            )

    def store_far(columns, value):
        far[:, columns] = value.astype(jnp.bfloat16)

    def store_right(columns, value):
        kept[0, :, columns] = value[:half]
        sent[0, low, columns] = value[half:].astype(jnp.bfloat16)

    def store_left(columns, value):
        kept[1, :, columns] = value[half:]
        sent[1, top, columns] = value[:half].astype(jnp.bfloat16)

    def store_own(columns, value):
        out_ref[:, columns] = value

    for load in loads:
        load.wait()
    multiply(2, store_far)
    ring[0].start()
    ring[1].start()
    multiply(1, store_right)
    ring[2].start()
    multiply(3, store_left)
    ring[3].start()
    for copy in square_copies:
        copy.start()
    multiply(0, store_own)
    for i, rows in ((0, top), (1, low)):
        ring[i].wait_recv()

        @pl.loop(0, steps)
        def _(j):
            columns = pl.ds(pl.multiple_of(j * step, step), step)
            sent[i, rows, columns] = (
                kept[i, :, columns] + relay[i, :, columns].astype(jnp.float32)
            ).astype(jnp.bfloat16)

        ring[4 + i].start()
    total = squares_ref[chip]
    for i, copy in enumerate(square_copies):
        copy.wait_recv()
        total += squares[i]
    inverse = lax.rsqrt(total[:, :1] / features + 1e-06)
    for i in range(2, 6):
        ring[i].wait_recv()

    @pl.loop(0, steps)
    def _(j):
        columns = pl.ds(pl.multiple_of(j * step, step), step)
        out_ref[:, columns] = (
            out_ref[:, columns]
            + final[0, :, columns].astype(jnp.float32)
            + final[1, :, columns].astype(jnp.float32)
        ) * inverse

    for copy in square_copies:
        copy.wait_send()
    for copy in ring:
        copy.wait_send()


def head_reduce(rows, squares, head_own, head_pair, collective_id):
    chips, count, _ = rows.shape
    width, columns = head_own.shape
    vmem = pl.BlockSpec(memory_space=pltpu.VMEM)
    hbm = pl.BlockSpec(memory_space=pl.ANY)
    return pl.pallas_call(
        head_kernel,
        out_shape=jax.ShapeDtypeStruct((count, columns), jnp.float32),
        in_specs=[vmem, vmem, hbm, hbm],
        out_specs=vmem,
        scratch_shapes=[
            pltpu.VMEM((width, columns), jnp.bfloat16),
            pltpu.VMEM((width, columns), jnp.bfloat16),
            pltpu.VMEM((count, columns), jnp.bfloat16),
            pltpu.VMEM((2, count // 2, columns), jnp.float32),
            pltpu.VMEM((2, count // 2, columns), jnp.bfloat16),
            pltpu.VMEM((2, count, columns), jnp.bfloat16),
            pltpu.VMEM((2, count, columns), jnp.bfloat16),
            pltpu.VMEM((3, count, 128), jnp.float32),
            pltpu.SemaphoreType.DMA((2,)),
            pltpu.SemaphoreType.DMA((6,)),
            pltpu.SemaphoreType.DMA((6,)),
            pltpu.SemaphoreType.DMA((3,)),
            pltpu.SemaphoreType.DMA((3,)),
        ],
        compiler_params=pltpu.CompilerParams(
            collective_id=collective_id, has_side_effects=True, vmem_limit_bytes=56 * 1024 * 1024
        ),
    )(rows, squares, head_own, head_pair)


def per_device(
    tokens_in,
    gate_raw,
    expert_ids,
    w_gate,
    w_up,
    w_down,
    final_gain,
    teacher_head,
    student_hidden,
    student_head,
    sampled_ids,
    token_weight,
):
    tok_count = lax.axis_size("tok")
    voc_count = lax.axis_size("voc")
    rows_here, top_k = expert_ids.shape
    model_width = tokens_in.shape[1]
    part_width = model_width // tok_count
    student_pair = lax.ppermute(student_head, "tok", [(i, i ^ 1) for i in range(tok_count)])
    teacher_pair = lax.ppermute(teacher_head, "tok", [(i, i ^ 1) for i in range(tok_count)])
    ids_shares = jnp.concatenate(
        [expert_ids.astype(jnp.float32), gate_raw, jnp.zeros((rows_here, 128 - 2 * top_k), jnp.float32)],
        axis=1,
    )
    rows_all = tok_count * rows_here
    student_all, tokens_all, table = exchange(
        [student_hidden, tokens_in, ids_shares],
        [
            (voc_count,) + student_hidden.shape,
            (tok_count, rows_here, model_width),
            (tok_count, rows_here, 128),
        ],
        ("voc", "tok", "tok"),
        2,
        targets=(at_peer, at_core_chip, at_core_chip),
    )
    student_part = jnp.dot(
        student_all.reshape(-1, part_width), student_head, preferred_element_type=jnp.float32
    )
    tokens_all = tokens_all.reshape(rows_all, model_width)
    table = table.reshape(rows_all, 128)
    slots = 2
    here = voc_count // 2
    column = jnp.arange(here * tok_count * slots, dtype=jnp.int32)
    column_expert = column // (tok_count * slots) + lax.axis_index("tok") * here
    column_block = column // slots % tok_count
    column_slot = column % slots
    row = jnp.arange(rows_all, dtype=jnp.int32)
    gates = table[:, top_k : 2 * top_k]
    shares = gates / jnp.sum(gates, axis=1, keepdims=True)
    named = [
        table[:, k : k + 1] == column_expert.astype(jnp.float32)[None, :] for k in range(top_k)
    ]
    present = functools.reduce(jnp.logical_or, named)
    share_of = sum(jnp.where(named[k], shares[:, k : k + 1], 0.0) for k in range(top_k))
    before = (row[:, None] // rows_here == row[None, :] // rows_here) & (row[None, :] < row[:, None])
    earlier = jnp.dot(
        before.astype(jnp.bfloat16), present.astype(jnp.bfloat16), preferred_element_type=jnp.float32
    )
    matched = (
        present
        & (earlier == column_slot.astype(jnp.float32)[None, :])
        & (row[:, None] // rows_here == column_block[None, :])
    )
    combine_table = jnp.where(matched, share_of, 0.0)
    dispatched = lax.dot_general(
        matched.astype(jnp.bfloat16),
        tokens_all,
        (((0,), (0,)), ((), ())),
        preferred_element_type=jnp.float32,
    ).astype(jnp.bfloat16)
    group = tok_count * slots
    dispatched, student_part = lax.optimization_barrier((dispatched, student_part))
    student_logits = lax.psum_scatter(student_part, "tok", scatter_dimension=0, tiled=True)
    returned = expert_layer(
        dispatched.reshape(here, group, model_width), w_gate, w_up, w_down, 3
    )
    pair_sum = jnp.sum(
        returned.astype(jnp.float32).reshape(here, 2, group, model_width), axis=1
    ).reshape(here * group, model_width)
    mix_part = jnp.dot(combine_table, pair_sum, precision=lax.Precision.HIGHEST)
    core_rows, chip_width = rows_all // 2, 2 * part_width
    (mix_parts,) = exchange(
        [mix_part.astype(jnp.bfloat16)],
        [(tok_count, core_rows, chip_width)],
        ("tok",),
        6,
        source=at_core_features,
    )
    tok_index = lax.axis_index("tok")
    feature_start = (tok_index // 2) * chip_width
    tokens_part = lax.dynamic_slice(
        tokens_all, ((tok_index % 2) * core_rows, feature_start), (core_rows, chip_width)
    )
    residual_sum = tokens_part.astype(jnp.float32) + jnp.sum(mix_parts.astype(jnp.float32), axis=0)
    squares = jnp.sum(residual_sum * residual_sum, axis=1, keepdims=True)
    gain_part = lax.dynamic_slice_in_dim(final_gain, feature_start, chip_width, 0)
    scaled = (residual_sum * gain_part[None, :]).astype(jnp.bfloat16)
    chips = tok_count // 2
    teacher_rows, squares_rows = exchange(
        [
            scaled.reshape(chips, rows_here, chip_width),
            jnp.broadcast_to(squares, (core_rows, 128)).reshape(chips, rows_here, 128),
        ],
        [
            (chips, voc_count, rows_here, chip_width),
            (chips, voc_count, rows_here, 128),
        ],
        ("voc", "voc"),
        8,
        targets=(at_second, at_second),
    )
    vocab_local = teacher_head.shape[1]
    teacher_logits = head_reduce(
        teacher_rows.reshape(chips, voc_count * rows_here, chip_width),
        squares_rows.reshape(chips, voc_count * rows_here, 128),
        teacher_head,
        teacher_pair,
        10,
    )
    differ = student_logits - teacher_logits
    vocab_start = lax.axis_index("voc") * vocab_local
    picked = sampled_ids[:, None] - vocab_start == jnp.arange(vocab_local, dtype=jnp.int32)[None, :]
    local_tmax = jnp.max(teacher_logits, axis=1)
    local_smax = jnp.max(student_logits, axis=1)
    student_exp = jnp.exp(student_logits - local_smax[:, None])
    stats = jnp.stack(
        [
            local_tmax,
            local_smax,
            jnp.sum(jnp.exp(teacher_logits - local_tmax[:, None]), axis=1),
            jnp.sum(student_exp, axis=1),
            jnp.sum(student_exp * differ, axis=1),
            jnp.sum(jnp.where(picked, student_logits, 0.0), axis=1),
            jnp.sum(jnp.where(picked, teacher_logits, 0.0), axis=1),
            jnp.zeros_like(local_tmax),
        ]
    )
    (every,) = exchange([stats], [(voc_count,) + stats.shape], ("voc",), 9)
    teacher_max = jnp.max(every[:, 0], axis=0)
    student_max = jnp.max(every[:, 1], axis=0)
    teacher_scale = jnp.exp(every[:, 0] - teacher_max[None, :])
    student_scale = jnp.exp(every[:, 1] - student_max[None, :])
    teacher_sum = jnp.sum(every[:, 2] * teacher_scale, axis=0)
    student_sum = jnp.sum(every[:, 3] * student_scale, axis=0)
    cross_sum = jnp.sum(every[:, 4] * student_scale, axis=0)
    picked_s = jnp.sum(every[:, 5], axis=0)
    picked_t = jnp.sum(every[:, 6], axis=0)
    teacher_norm = teacher_max + jnp.log(teacher_sum)
    student_norm = student_max + jnp.log(student_sum)
    expect = cross_sum / student_sum
    token_loss = (
        expect - student_norm + teacher_norm + (picked_s - student_norm) - (picked_t - teacher_norm)
    )
    student_prob = jnp.exp(student_logits - student_norm[:, None])
    logit_grad = (
        token_weight[:, None]
        * (student_prob * (differ - expect[:, None]) + picked.astype(jnp.float32) - student_prob)
    ).astype(jnp.bfloat16)
    hidden_grad = grad_reduce(logit_grad, student_head, student_pair, 4)
    return (token_loss, hidden_grad)


def solution(mesh):
    in_specs = (
        P(("tok", "voc"), None),
        P(("tok", "voc"), None),
        P(("tok", "voc"), None),
        P(None, ("tok", "voc")),
        P(None, ("tok", "voc")),
        P(("tok", "voc"), None),
        P(),
        P("tok", "voc"),
        P("voc", "tok"),
        P("tok", "voc"),
        P("tok"),
        P("tok"),
    )
    out_specs = (P("tok"), P("voc", "tok"))
    return jax.shard_map(
        per_device, mesh=mesh, in_specs=in_specs, out_specs=out_specs, check_vma=False
    )
```

```python
import functools
import jax
import jax.numpy as jnp
from jax import lax
from jax.experimental import pallas as pl
from jax.experimental.pallas import tpu as pltpu
from jax.sharding import PartitionSpec as P

MESH = pl.DeviceIdType.MESH


def device_on(axis, index):
    if axis == "tok":
        return (index, lax.axis_index("voc"))
    return (lax.axis_index("tok"), index)


def exchange_kernel(axes, sizes, source, targets, *refs):
    count = len(axes)
    ins, outs = refs[:count], refs[count : 2 * count]
    send_sem, recv_sem, own_sem = refs[2 * count :]
    barrier = pltpu.get_barrier_semaphore()
    for axis in sorted(set(axes)):
        n = sizes[axis]

        @pl.loop(1, n)
        def _(k):
            peer = lax.rem(lax.axis_index(axis) + k, n)
            pl.semaphore_signal(barrier, inc=1, device_id=device_on(axis, peer), device_id_type=MESH)

    pl.semaphore_wait(barrier, sum(sizes[axis] - 1 for axis in set(axes)))

    def copy(i, k, back):
        me, n = lax.axis_index(axes[i]), sizes[axes[i]]
        peer = lax.rem(me + k, n)
        return pltpu.make_async_remote_copy(
            src_ref=source(ins[i], peer),
            dst_ref=targets[i](outs[i], lax.rem(me - k + n, n) if back else me),
            send_sem=send_sem.at[i, k],
            recv_sem=recv_sem.at[i, k],
            device_id=device_on(axes[i], peer),
            device_id_type=MESH,
        )

    for i in range(count):

        @pl.loop(1, sizes[axes[i]])
        def _(k):
            copy(i, k, False).start()

    for i in range(count):
        me = lax.axis_index(axes[i])
        own = pltpu.make_async_copy(source(ins[i], me), targets[i](outs[i], me), own_sem)
        own.start()
        own.wait()

    for i in range(count):

        @pl.loop(1, sizes[axes[i]])
        def _(k):
            copy(i, k, True).wait()


def whole(ref, peer):
    return ref


def at_peer(ref, peer):
    return ref.at[peer]


def at_pair(ref, peer):
    return ref.at[peer // 2]


def at_second(ref, peer):
    return ref.at[:, peer]


def at_core_chip(ref, peer):
    return ref.at[lax.rem(peer, 2) * 4 + peer // 2]


def at_core_features(ref, peer):
    rows = pl.ds(pl.multiple_of(lax.rem(peer, 2) * 32, 32), 32)
    return ref.at[rows, pl.ds(pl.multiple_of((peer // 2) * 1024, 1024), 1024)]


def exchange(arrays, shapes, axes, collective_id, source=whole, targets=None):
    count = len(arrays)
    sizes = {axis: lax.axis_size(axis) for axis in axes}
    return pl.pallas_call(
        functools.partial(
            exchange_kernel, axes, sizes, source, targets or (at_peer,) * count
        ),
        out_shape=[jax.ShapeDtypeStruct(o, x.dtype) for o, x in zip(shapes, arrays)],
        in_specs=[pl.BlockSpec(memory_space=pltpu.VMEM)] * count,
        out_specs=[pl.BlockSpec(memory_space=pltpu.VMEM)] * count,
        scratch_shapes=[
            pltpu.SemaphoreType.DMA((count, max(sizes.values()))),
            pltpu.SemaphoreType.DMA((count, max(sizes.values()))),
            pltpu.SemaphoreType.DMA,
        ],
        compiler_params=pltpu.CompilerParams(collective_id=collective_id, has_side_effects=True),
    )(*arrays)


OFFSETS = (
    (0, 1), (1, 0), (0, 3), (3, 0), (1, 1), (3, 3), (1, 3),
    (3, 1), (2, 0), (0, 2), (1, 2), (2, 1), (3, 2), (2, 3), (2, 2),
)


def expert_kernel(
    x_ref, gate_hbm, up_hbm, down_hbm, out_ref,
    gate_w, up_w, down_w, rows, results,
    load_sem, rows_send, rows_recv, back_send, back_recv, own_sem,
):
    v = lax.axis_index("voc")
    y, z = v // 4, lax.rem(v, 4)
    loads = [
        pltpu.make_async_copy(source, target, load_sem.at[i])
        for i, (source, target) in enumerate(
            ((gate_hbm, gate_w), (up_hbm, up_w), (down_hbm, down_w))
        )
    ]
    for load in loads:
        load.start()

    def ahead(i):
        dy, dz = OFFSETS[i - 1]
        return lax.rem(y + dy, 4) * 4 + lax.rem(z + dz, 4)

    def behind(i):
        dy, dz = OFFSETS[i - 1]
        return lax.rem(y + 4 - dy, 4) * 4 + lax.rem(z + 4 - dz, 4)

    barrier = pltpu.get_barrier_semaphore()
    for i in range(1, 16):
        pl.semaphore_signal(
            barrier, inc=1, device_id=device_on("voc", ahead(i)), device_id_type=MESH
        )
    pl.semaphore_wait(barrier, 15)

    def row_copy(i):
        return pltpu.make_async_remote_copy(
            src_ref=x_ref.at[ahead(i) // 2],
            dst_ref=rows.at[i],
            send_sem=rows_send.at[i],
            recv_sem=rows_recv.at[i],
            device_id=device_on("voc", ahead(i)),
            device_id_type=MESH,
        )

    def back_copy(i, place):
        return pltpu.make_async_remote_copy(
            src_ref=results.at[i],
            dst_ref=out_ref.at[place],
            send_sem=back_send.at[i],
            recv_sem=back_recv.at[i],
            device_id=device_on("voc", behind(i)),
            device_id_type=MESH,
        )

    for i in range(1, 16):
        row_copy(i).start()
    own = pltpu.make_async_copy(x_ref.at[v // 2], rows.at[0], own_sem.at[0])
    own.start()
    for load in loads:
        load.wait()
    own.wait()
    group, width = rows.shape[1:]
    step = 512
    own_back = pltpu.make_async_copy(results.at[0], out_ref.at[v], own_sem.at[1])
    for first in (0, 8):
        for i in range(max(first, 1), first + 8):
            row_copy(i).wait_recv()
        batch = rows[pl.ds(first, 8)].reshape(8 * group, width)
        gate = jnp.dot(batch, gate_w[...], preferred_element_type=jnp.float32)
        up = jnp.dot(batch, up_w[...], preferred_element_type=jnp.float32)
        units = (gate * jax.nn.sigmoid(gate) * up).astype(jnp.bfloat16)

        @pl.loop(0, width // step)
        def _(j):
            columns = pl.ds(pl.multiple_of(j * step, step), step)
            part = jnp.dot(units, down_w[:, columns], preferred_element_type=jnp.float32)
            results[pl.ds(first, 8), :, columns] = part.astype(jnp.bfloat16).reshape(8, group, step)

        for i in range(max(first, 1), first + 8):
            back_copy(i, v).start()
        if first == 0:
            own_back.start()
    own_back.wait()
    for i in range(1, 16):
        row_copy(i).wait_send()
        back_copy(i, ahead(i)).wait()


def expert_layer(x, w_gate, w_up, w_down, collective_id):
    _, group, width = x.shape
    vmem = pl.BlockSpec(memory_space=pltpu.VMEM)
    hbm = pl.BlockSpec(memory_space=pl.ANY)
    return pl.pallas_call(
        expert_kernel,
        out_shape=jax.ShapeDtypeStruct((16, group, width), jnp.bfloat16),
        in_specs=[vmem, hbm, hbm, hbm],
        out_specs=vmem,
        scratch_shapes=[
            pltpu.VMEM(w_gate.shape, jnp.bfloat16),
            pltpu.VMEM(w_up.shape, jnp.bfloat16),
            pltpu.VMEM(w_down.shape, jnp.bfloat16),
            pltpu.VMEM((16, group, width), jnp.bfloat16),
            pltpu.VMEM((16, group, width), jnp.bfloat16),
            pltpu.SemaphoreType.DMA((3,)),
            pltpu.SemaphoreType.DMA((16,)),
            pltpu.SemaphoreType.DMA((16,)),
            pltpu.SemaphoreType.DMA((16,)),
            pltpu.SemaphoreType.DMA((16,)),
            pltpu.SemaphoreType.DMA((2,)),
        ],
        compiler_params=pltpu.CompilerParams(
            collective_id=collective_id, has_side_effects=True, vmem_limit_bytes=56 * 1024 * 1024
        ),
    )(x, w_gate, w_up, w_down)


def loss_kernel(
    rows_ref, squares_ref, ids_ref, weight_ref,
    head_own_hbm, head_pair_hbm, own_hbm, pair_hbm, student_hbm,
    loss_ref, out_ref,
    head_own, head_pair, own_w, pair_w, student,
    far, kept, relay, sent, final, squares, logits,
    columns_stat, stat, stats, grads, blocks, terms, landed,
    load_sem, head_send, head_recv, square_send, square_recv, stat_send, stat_recv,
    ring_send, ring_recv, term_send, term_recv, self_sem,
):
    t, v = lax.axis_index("tok"), lax.axis_index("voc")
    core = lax.rem(t, 2)
    chip = t // 2
    partner = t + 1 - 2 * core
    right, left, across = lax.rem(t + 2, 8), lax.rem(t + 6, 8), lax.rem(t + 4, 8)
    count, vocab = grads.shape
    half = count // 2
    source_core = lax.rem(v // 2, 2)
    width = own_w.shape[0]
    features = rows_ref.shape[2] * 4
    step = 256
    steps = vocab // step
    top, low = pl.ds(0, half), pl.ds(half, half)
    loads = [
        pltpu.make_async_copy(source, target, load_sem.at[i])
        for i, (source, target) in enumerate(
            (
                (head_own_hbm, head_own),
                (head_pair_hbm, head_pair),
                (student_hbm, student),
                (own_hbm, own_w),
                (pair_hbm, pair_w),
            )
        )
    ]
    for load in loads[:2]:
        load.start()
    barrier = pltpu.get_barrier_semaphore()
    for side in (right, left, across):
        pl.semaphore_signal(barrier, inc=1, device_id=(side, v), device_id_type=MESH)

    @pl.loop(0, 16)
    def _(k):
        pl.semaphore_signal(barrier, inc=1, device_id=(partner, k), device_id_type=MESH)

    @pl.loop(1, 16)
    def _(k):
        pl.semaphore_signal(
            barrier, inc=1, device_id=(t, lax.rem(v + k, 16)), device_id_type=MESH
        )

    pl.semaphore_wait(barrier, 34)

    chips = [lax.rem(chip + shift, 4) for shift in range(4)]
    square_copies = [
        pltpu.make_async_remote_copy(
            src_ref=squares_ref.at[chips[shift]],
            dst_ref=squares.at[shift - 1],
            send_sem=square_send.at[shift - 1],
            recv_sem=square_recv.at[shift - 1],
            device_id=(device, v),
            device_id_type=MESH,
        )
        for shift, device in ((1, right), (2, across), (3, left))
    ]
    head_plan = (
        (far.at[top], relay.at[0], right),
        (far.at[low], relay.at[1], left),
        (sent.at[0, low], final.at[0, low], right),
        (sent.at[1, top], final.at[1, top], left),
        (sent.at[0, top], final.at[0, top], right),
        (sent.at[1, low], final.at[1, low], left),
    )
    head_ring = [
        pltpu.make_async_remote_copy(
            src_ref=source,
            dst_ref=target,
            send_sem=head_send.at[i],
            recv_sem=head_recv.at[i],
            device_id=(device, v),
            device_id_type=MESH,
        )
        for i, (source, target, device) in enumerate(head_plan)
    ]
    own_columns = pl.ds(pl.multiple_of(core * width, width), width)
    pair_columns = pl.ds(pl.multiple_of((1 - core) * width, width), width)

    def head_part(shift, store):
        own_rows = rows_ref[chips[shift], :, own_columns]
        pair_rows = rows_ref[chips[shift], :, pair_columns]

        @pl.loop(0, steps)
        def _(j):
            columns = pl.ds(pl.multiple_of(j * step, step), step)
            store(
                columns,
                jnp.dot(own_rows, head_own[:, columns], preferred_element_type=jnp.float32)
                + jnp.dot(pair_rows, head_pair[:, columns], preferred_element_type=jnp.float32),
            )

    def store_far(columns, value):
        far[:, columns] = value.astype(jnp.bfloat16)

    def store_right(columns, value):
        kept[0, :, columns] = value[:half]
        sent[0, low, columns] = value[half:].astype(jnp.bfloat16)

    def store_left(columns, value):
        kept[1, :, columns] = value[half:]
        sent[1, top, columns] = value[:half].astype(jnp.bfloat16)

    def store_own(columns, value):
        logits[:, columns] = value

    for load in loads[:2]:
        load.wait()
    for load in loads[2:]:
        load.start()
    head_part(2, store_far)
    head_ring[0].start()
    head_ring[1].start()
    head_part(1, store_right)
    head_ring[2].start()
    head_part(3, store_left)
    head_ring[3].start()
    for copy in square_copies:
        copy.start()
    head_part(0, store_own)
    for i, rows in ((0, top), (1, low)):
        head_ring[i].wait_recv()

        @pl.loop(0, steps)
        def _(j):
            columns = pl.ds(pl.multiple_of(j * step, step), step)
            sent[i, rows, columns] = (
                kept[i, :, columns] + relay[i, :, columns].astype(jnp.float32)
            ).astype(jnp.bfloat16)

        head_ring[4 + i].start()
    total = squares_ref[chip]
    for i, copy in enumerate(square_copies):
        copy.wait_recv()
        total += squares[i]
    inverse = lax.rsqrt(total[:, :1] / features + 1e-06)
    for load in loads[2:]:
        load.wait()
    for i in range(2, 6):
        head_ring[i].wait_recv()

    lanes = 128
    lane = lax.broadcasted_iota(jnp.int32, (half, lanes), 1)
    start = v * vocab

    for part in (top, low):
        scale = inverse[part.start : part.start + half]
        target = ids_ref[part, :][:, :1] - start

        def largest(j, carry):
            at = pl.ds(pl.multiple_of(j * lanes, lanes), lanes)
            value = (
                logits[part, at]
                + final[0, part, at].astype(jnp.float32)
                + final[1, part, at].astype(jnp.float32)
            ) * scale
            logits[part, at] = value
            return jnp.maximum(carry[0], value), jnp.maximum(carry[1], student[part, at])

        lowest = jnp.full((half, lanes), -jnp.inf, jnp.float32)
        teacher_max, student_max = lax.fori_loop(0, vocab // lanes, largest, (lowest, lowest))
        teacher_max = jnp.max(teacher_max, axis=1, keepdims=True)
        student_max = jnp.max(student_max, axis=1, keepdims=True)

        def sums(j, carry):
            at = pl.ds(pl.multiple_of(j * lanes, lanes), lanes)
            teacher, own = logits[part, at], student[part, at]
            weight = jnp.exp(own - student_max)
            picked = lane + j * lanes == target
            return (
                carry[0] + jnp.exp(teacher - teacher_max),
                carry[1] + weight,
                carry[2] + weight * (own - teacher),
                carry[3] + jnp.where(picked, own, 0.0),
                carry[4] + jnp.where(picked, teacher, 0.0),
            )

        totals = lax.fori_loop(
            0, vocab // lanes, sums, (jnp.zeros((half, lanes), jnp.float32),) * 5
        )
        table = jnp.where(lane == 0, teacher_max, jnp.where(lane == 1, student_max, 0.0))
        for i, total in enumerate(totals):
            table = jnp.where(lane == i + 2, jnp.sum(total, axis=1, keepdims=True), table)
        columns_stat[part, :] = table

    stat[...] = jnp.transpose(columns_stat[...])[:8]

    def stat_copy(k, sender):
        return pltpu.make_async_remote_copy(
            src_ref=stat,
            dst_ref=stats.at[sender],
            send_sem=stat_send.at[k],
            recv_sem=stat_recv.at[k],
            device_id=(t, lax.rem(v + k, 16)),
            device_id_type=MESH,
        )

    @pl.loop(1, 16)
    def _(k):
        stat_copy(k, v).start()

    stats[v] = stat[...]

    @pl.loop(1, 16)
    def _(k):
        stat_copy(k, lax.rem(v - k + 16, 16)).wait()

    every = [stats[:, pl.ds(i, 1), :] for i in range(7)]
    teacher_max = jnp.max(every[0], axis=0)
    student_max = jnp.max(every[1], axis=0)
    teacher_sum = jnp.sum(every[2] * jnp.exp(every[0] - teacher_max), axis=0)
    student_scale = jnp.exp(every[1] - student_max)
    student_sum = jnp.sum(every[3] * student_scale, axis=0)
    expect = jnp.sum(every[4] * student_scale, axis=0) / student_sum
    teacher_norm = teacher_max + jnp.log(teacher_sum)
    student_norm = student_max + jnp.log(student_sum)
    loss_ref[...] = (
        expect
        - student_norm
        + teacher_norm
        + (jnp.sum(every[5], axis=0) - student_norm)
        - (jnp.sum(every[6], axis=0) - teacher_norm)
    )
    sublane = lax.broadcasted_iota(jnp.int32, (lanes, lanes), 0)
    columns_stat[...] = jnp.transpose(
        jnp.where(sublane == 0, student_norm, jnp.where(sublane == 1, expect, 0.0))
    )
    for part in (top, low):
        norm = columns_stat[part, :][:, 0:1]
        mean = columns_stat[part, :][:, 1:2]
        scale = weight_ref[part, :][:, :1]
        target = ids_ref[part, :][:, :1] - start

        @pl.loop(0, vocab // lanes)
        def _(j):
            at = pl.ds(pl.multiple_of(j * lanes, lanes), lanes)
            own = student[part, at]
            prob = jnp.exp(own - norm)
            picked = (lane + j * lanes == target).astype(jnp.float32)
            grads[part, at] = (
                scale * (prob * (own - logits[part, at] - mean) + picked - prob)
            ).astype(jnp.bfloat16)

    for copy in square_copies:
        copy.wait_send()
    for copy in head_ring:
        copy.wait_send()

    plan = (
        (grads.at[top], blocks.at[0, top], right),
        (grads.at[low], blocks.at[0, low], right),
        (grads.at[low], blocks.at[1, low], left),
        (grads.at[top], blocks.at[1, top], left),
        (blocks.at[0, top], blocks.at[2, top], right),
        (blocks.at[1, low], blocks.at[2, low], left),
    )
    ring = [
        pltpu.make_async_remote_copy(
            src_ref=source,
            dst_ref=target,
            send_sem=ring_send.at[i],
            recv_sem=ring_recv.at[i],
            device_id=(device, v),
            device_id_type=MESH,
        )
        for i, (source, target, device) in enumerate(plan)
    ]
    for i in (0, 2, 1, 3):
        ring[i].start()

    def term_copy(slot, side, h, piece):
        return pltpu.make_async_remote_copy(
            src_ref=terms.at[slot, side, pl.ds(h * half, half)],
            dst_ref=landed.at[v],
            send_sem=term_send.at[slot * 4 + side * 2 + h],
            recv_sem=term_recv.at[v],
            device_id=(partner if side else t, piece),
            device_id_type=MESH,
        )

    def self_copy(slot, h):
        return pltpu.make_async_copy(
            terms.at[slot, 0, pl.ds(h * half, half)], landed.at[v], self_sem
        )

    pieces = [
        [lax.rem(chip + shift, 4) * 4 + 2 * core + h for h in range(2)] for shift in (0, 3, 1, 2)
    ]

    def multiply(slot, block):
        for side, weight in enumerate((own_w, pair_w)):
            terms[slot, side] = lax.dot_general(
                block[...], weight[...], (((1,), (1,)), ((), ())), preferred_element_type=jnp.float32
            ).astype(jnp.bfloat16)
            for h in range(2):
                piece = pieces[slot][h]
                if side:
                    term_copy(slot, side, h, piece).start()
                else:
                    pl.when(piece != v)(term_copy(slot, side, h, piece).start)
                    pl.when(piece == v)(self_copy(slot, h).start)

    multiply(0, grads)
    ring[0].wait_recv()
    ring[4].start()
    ring[2].wait_recv()
    ring[5].start()
    ring[1].wait_recv()
    multiply(1, blocks.at[0])
    ring[3].wait_recv()
    multiply(2, blocks.at[1])
    ring[4].wait_recv()
    ring[5].wait_recv()
    multiply(3, blocks.at[2])

    for slot in range(4):
        for h in range(2):
            piece = pieces[slot][h]
            term_copy(slot, 1, h, piece).wait_send()
            pl.when(piece != v)(term_copy(slot, 0, h, piece).wait_send)
            pl.when(piece == v)(self_copy(slot, h).wait)
    for copy in ring:
        copy.wait_send()

    @pl.loop(0, 16)
    def _(k):
        @pl.when(jnp.logical_or(source_core != core, k != v))
        def _():
            pltpu.make_async_remote_copy(
                src_ref=terms.at[0, 0, top],
                dst_ref=landed.at[k],
                send_sem=term_send.at[0],
                recv_sem=term_recv.at[k],
                device_id=(partner, v),
                device_id_type=MESH,
            ).wait_recv()

    total = landed[0].astype(jnp.float32)
    for k in range(1, 16):
        total += landed[k].astype(jnp.float32)
    out_ref[...] = total.astype(out_ref.dtype)


def loss_and_grad(
    rows, squares, ids, weight, head_own, head_pair, own, pair, student, collective_id
):
    _, count, _ = rows.shape
    width, vocab = head_own.shape
    vmem = pl.BlockSpec(memory_space=pltpu.VMEM)
    hbm = pl.BlockSpec(memory_space=pl.ANY)
    bf16, f32 = jnp.bfloat16, jnp.float32
    dma = pltpu.SemaphoreType.DMA
    return pl.pallas_call(
        loss_kernel,
        out_shape=(
            jax.ShapeDtypeStruct((1, count), f32),
            jax.ShapeDtypeStruct((count // 2, width), bf16),
        ),
        in_specs=[vmem] * 4 + [hbm] * 5,
        out_specs=(vmem, vmem),
        scratch_shapes=[pltpu.VMEM((width, vocab), bf16)] * 4
        + [
            pltpu.VMEM((count, vocab), f32),
            pltpu.VMEM((count, vocab), bf16),
            pltpu.VMEM((2, count // 2, vocab), f32),
            pltpu.VMEM((2, count // 2, vocab), bf16),
            pltpu.VMEM((2, count, vocab), bf16),
            pltpu.VMEM((2, count, vocab), bf16),
            pltpu.VMEM((3, count, 128), f32),
            pltpu.VMEM((count, vocab), f32),
            pltpu.VMEM((count, 128), f32),
            pltpu.VMEM((8, count), f32),
            pltpu.VMEM((16, 8, count), f32),
            pltpu.VMEM((count, vocab), bf16),
            pltpu.VMEM((3, count, vocab), bf16),
            pltpu.VMEM((4, 2, count, width), bf16),
            pltpu.VMEM((16, count // 2, width), bf16),
            dma((5,)),
            dma((6,)),
            dma((6,)),
            dma((3,)),
            dma((3,)),
            dma((16,)),
            dma((16,)),
            dma((6,)),
            dma((6,)),
            dma((16,)),
            dma((16,)),
            dma,
        ],
        compiler_params=pltpu.CompilerParams(
            collective_id=collective_id, has_side_effects=True, vmem_limit_bytes=60 * 1024 * 1024
        ),
    )(rows, squares, ids, weight, head_own, head_pair, own, pair, student)


def per_device(
    tokens_in,
    gate_raw,
    expert_ids,
    w_gate,
    w_up,
    w_down,
    final_gain,
    teacher_head,
    student_hidden,
    student_head,
    sampled_ids,
    token_weight,
):
    tok_count = lax.axis_size("tok")
    voc_count = lax.axis_size("voc")
    rows_here, top_k = expert_ids.shape
    model_width = tokens_in.shape[1]
    part_width = model_width // tok_count
    student_pair = lax.ppermute(student_head, "tok", [(i, i ^ 1) for i in range(tok_count)])
    teacher_pair = lax.ppermute(teacher_head, "tok", [(i, i ^ 1) for i in range(tok_count)])
    ids_shares = jnp.concatenate(
        [expert_ids.astype(jnp.float32), gate_raw, jnp.zeros((rows_here, 128 - 2 * top_k), jnp.float32)],
        axis=1,
    )
    rows_all = tok_count * rows_here
    student_all, tokens_all, table = exchange(
        [student_hidden, tokens_in, ids_shares],
        [
            (voc_count,) + student_hidden.shape,
            (tok_count, rows_here, model_width),
            (tok_count, rows_here, 128),
        ],
        ("voc", "tok", "tok"),
        2,
        targets=(at_peer, at_core_chip, at_core_chip),
    )
    student_part = jnp.dot(
        student_all.reshape(-1, part_width), student_head, preferred_element_type=jnp.float32
    )
    tokens_all = tokens_all.reshape(rows_all, model_width)
    table = table.reshape(rows_all, 128)
    slots = 2
    here = voc_count // 2
    column = jnp.arange(here * tok_count * slots, dtype=jnp.int32)
    column_expert = column // (tok_count * slots) + lax.axis_index("tok") * here
    column_block = column // slots % tok_count
    column_slot = column % slots
    row = jnp.arange(rows_all, dtype=jnp.int32)
    gates = table[:, top_k : 2 * top_k]
    shares = gates / jnp.sum(gates, axis=1, keepdims=True)
    named = [
        table[:, k : k + 1] == column_expert.astype(jnp.float32)[None, :] for k in range(top_k)
    ]
    present = functools.reduce(jnp.logical_or, named)
    share_of = sum(jnp.where(named[k], shares[:, k : k + 1], 0.0) for k in range(top_k))
    before = (row[:, None] // rows_here == row[None, :] // rows_here) & (row[None, :] < row[:, None])
    earlier = jnp.dot(
        before.astype(jnp.bfloat16), present.astype(jnp.bfloat16), preferred_element_type=jnp.float32
    )
    matched = (
        present
        & (earlier == column_slot.astype(jnp.float32)[None, :])
        & (row[:, None] // rows_here == column_block[None, :])
    )
    combine_table = jnp.where(matched, share_of, 0.0)
    dispatched = lax.dot_general(
        matched.astype(jnp.bfloat16),
        tokens_all,
        (((0,), (0,)), ((), ())),
        preferred_element_type=jnp.float32,
    ).astype(jnp.bfloat16)
    group = tok_count * slots
    dispatched, student_part = lax.optimization_barrier((dispatched, student_part))
    student_logits = lax.psum_scatter(student_part, "tok", scatter_dimension=0, tiled=True)
    returned = expert_layer(
        dispatched.reshape(here, group, model_width), w_gate, w_up, w_down, 3
    )
    pair_sum = jnp.sum(
        returned.astype(jnp.float32).reshape(here, 2, group, model_width), axis=1
    ).reshape(here * group, model_width)
    mix_part = jnp.dot(combine_table, pair_sum, precision=lax.Precision.HIGHEST)
    core_rows, chip_width = rows_all // 2, 2 * part_width
    (mix_parts,) = exchange(
        [mix_part.astype(jnp.bfloat16)],
        [(tok_count, core_rows, chip_width)],
        ("tok",),
        6,
        source=at_core_features,
    )
    tok_index = lax.axis_index("tok")
    feature_start = (tok_index // 2) * chip_width
    tokens_part = lax.dynamic_slice(
        tokens_all, ((tok_index % 2) * core_rows, feature_start), (core_rows, chip_width)
    )
    residual_sum = tokens_part.astype(jnp.float32) + jnp.sum(mix_parts.astype(jnp.float32), axis=0)
    squares = jnp.sum(residual_sum * residual_sum, axis=1, keepdims=True)
    gain_part = lax.dynamic_slice_in_dim(final_gain, feature_start, chip_width, 0)
    scaled = (residual_sum * gain_part[None, :]).astype(jnp.bfloat16)
    chips = tok_count // 2
    teacher_rows, squares_rows = exchange(
        [
            scaled.reshape(chips, rows_here, chip_width),
            jnp.broadcast_to(squares, (core_rows, 128)).reshape(chips, rows_here, 128),
        ],
        [
            (chips, voc_count, rows_here, chip_width),
            (chips, voc_count, rows_here, 128),
        ],
        ("voc", "voc"),
        8,
        targets=(at_second, at_second),
    )
    token_count = sampled_ids.shape[0]
    token_loss, hidden_grad = loss_and_grad(
        teacher_rows.reshape(chips, token_count, chip_width),
        squares_rows.reshape(chips, token_count, 128),
        jnp.broadcast_to(sampled_ids[:, None], (token_count, 128)),
        jnp.broadcast_to(token_weight[:, None], (token_count, 128)),
        teacher_head,
        teacher_pair,
        student_head,
        student_pair,
        student_logits,
        10,
    )
    token_loss = token_loss.reshape(token_count)
    return (token_loss, hidden_grad)


def solution(mesh):
    in_specs = (
        P(("tok", "voc"), None),
        P(("tok", "voc"), None),
        P(("tok", "voc"), None),
        P(None, ("tok", "voc")),
        P(None, ("tok", "voc")),
        P(("tok", "voc"), None),
        P(),
        P("tok", "voc"),
        P("voc", "tok"),
        P("tok", "voc"),
        P("tok"),
        P("tok"),
    )
    out_specs = (P("tok"), P("voc", "tok"))
    return jax.shard_map(
        per_device, mesh=mesh, in_specs=in_specs, out_specs=out_specs, check_vma=False
    )
```

```python
import functools
import jax
import jax.numpy as jnp
from jax import lax
from jax.experimental import pallas as pl
from jax.experimental.pallas import tpu as pltpu
from jax.sharding import PartitionSpec as P

MESH = pl.DeviceIdType.MESH


def device_on(axis, index):
    if axis == "tok":
        return (index, lax.axis_index("voc"))
    return (lax.axis_index("tok"), index)


def exchange_kernel(axes, sizes, source, targets, *refs):
    count = len(axes)
    ins, outs = refs[:count], refs[count : 2 * count]
    send_sem, recv_sem, own_sem = refs[2 * count :]
    barrier = pltpu.get_barrier_semaphore()
    for axis in sorted(set(axes)):
        n = sizes[axis]

        @pl.loop(1, n)
        def _(k):
            peer = lax.rem(lax.axis_index(axis) + k, n)
            pl.semaphore_signal(barrier, inc=1, device_id=device_on(axis, peer), device_id_type=MESH)

    pl.semaphore_wait(barrier, sum(sizes[axis] - 1 for axis in set(axes)))

    def copy(i, k, back):
        me, n = lax.axis_index(axes[i]), sizes[axes[i]]
        peer = lax.rem(me + k, n)
        return pltpu.make_async_remote_copy(
            src_ref=source(ins[i], peer),
            dst_ref=targets[i](outs[i], lax.rem(me - k + n, n) if back else me),
            send_sem=send_sem.at[i, k],
            recv_sem=recv_sem.at[i, k],
            device_id=device_on(axes[i], peer),
            device_id_type=MESH,
        )

    for i in range(count):

        @pl.loop(1, sizes[axes[i]])
        def _(k):
            copy(i, k, False).start()

    for i in range(count):
        me = lax.axis_index(axes[i])
        own = pltpu.make_async_copy(source(ins[i], me), targets[i](outs[i], me), own_sem)
        own.start()
        own.wait()

    for i in range(count):

        @pl.loop(1, sizes[axes[i]])
        def _(k):
            copy(i, k, True).wait()


def whole(ref, peer):
    return ref


def at_peer(ref, peer):
    return ref.at[peer]


def at_pair(ref, peer):
    return ref.at[peer // 2]


def at_second(ref, peer):
    return ref.at[:, peer]


def at_core_chip(ref, peer):
    return ref.at[lax.rem(peer, 2) * 4 + peer // 2]


def at_core_features(ref, peer):
    rows = pl.ds(pl.multiple_of(lax.rem(peer, 2) * 32, 32), 32)
    return ref.at[rows, pl.ds(pl.multiple_of((peer // 2) * 1024, 1024), 1024)]


def exchange(arrays, shapes, axes, collective_id, source=whole, targets=None):
    count = len(arrays)
    sizes = {axis: lax.axis_size(axis) for axis in axes}
    return pl.pallas_call(
        functools.partial(
            exchange_kernel, axes, sizes, source, targets or (at_peer,) * count
        ),
        out_shape=[jax.ShapeDtypeStruct(o, x.dtype) for o, x in zip(shapes, arrays)],
        in_specs=[pl.BlockSpec(memory_space=pltpu.VMEM)] * count,
        out_specs=[pl.BlockSpec(memory_space=pltpu.VMEM)] * count,
        scratch_shapes=[
            pltpu.SemaphoreType.DMA((count, max(sizes.values()))),
            pltpu.SemaphoreType.DMA((count, max(sizes.values()))),
            pltpu.SemaphoreType.DMA,
        ],
        compiler_params=pltpu.CompilerParams(collective_id=collective_id, has_side_effects=True),
    )(*arrays)


OFFSETS = (
    (0, 1), (1, 0), (0, 3), (3, 0), (1, 1), (3, 3), (1, 3),
    (3, 1), (2, 0), (0, 2), (1, 2), (2, 1), (3, 2), (2, 3), (2, 2),
)


def expert_kernel(
    x_ref, gate_hbm, up_hbm, down_hbm, out_ref,
    gate_w, up_w, down_w, rows, results,
    load_sem, rows_send, rows_recv, back_send, back_recv, own_sem,
):
    v = lax.axis_index("voc")
    y, z = v // 4, lax.rem(v, 4)
    loads = [
        pltpu.make_async_copy(source, target, load_sem.at[i])
        for i, (source, target) in enumerate(
            ((gate_hbm, gate_w), (up_hbm, up_w), (down_hbm, down_w))
        )
    ]
    for load in loads:
        load.start()

    def ahead(i):
        dy, dz = OFFSETS[i - 1]
        return lax.rem(y + dy, 4) * 4 + lax.rem(z + dz, 4)

    def behind(i):
        dy, dz = OFFSETS[i - 1]
        return lax.rem(y + 4 - dy, 4) * 4 + lax.rem(z + 4 - dz, 4)

    barrier = pltpu.get_barrier_semaphore()
    for i in range(1, 16):
        pl.semaphore_signal(
            barrier, inc=1, device_id=device_on("voc", ahead(i)), device_id_type=MESH
        )
    pl.semaphore_wait(barrier, 15)

    def row_copy(i):
        return pltpu.make_async_remote_copy(
            src_ref=x_ref.at[ahead(i) // 2],
            dst_ref=rows.at[i],
            send_sem=rows_send.at[i],
            recv_sem=rows_recv.at[i],
            device_id=device_on("voc", ahead(i)),
            device_id_type=MESH,
        )

    def back_copy(i, place):
        return pltpu.make_async_remote_copy(
            src_ref=results.at[i],
            dst_ref=out_ref.at[place],
            send_sem=back_send.at[i],
            recv_sem=back_recv.at[i],
            device_id=device_on("voc", behind(i)),
            device_id_type=MESH,
        )

    for i in range(1, 16):
        row_copy(i).start()
    own = pltpu.make_async_copy(x_ref.at[v // 2], rows.at[0], own_sem.at[0])
    own.start()
    for load in loads:
        load.wait()
    own.wait()
    group, width = rows.shape[1:]
    step = 512
    own_back = pltpu.make_async_copy(results.at[0], out_ref.at[v], own_sem.at[1])
    for first in (0, 8):
        for i in range(max(first, 1), first + 8):
            row_copy(i).wait_recv()
        batch = rows[pl.ds(first, 8)].reshape(8 * group, width)
        gate = jnp.dot(batch, gate_w[...], preferred_element_type=jnp.float32)
        up = jnp.dot(batch, up_w[...], preferred_element_type=jnp.float32)
        units = (gate * jax.nn.sigmoid(gate) * up).astype(jnp.bfloat16)

        @pl.loop(0, width // step)
        def _(j):
            columns = pl.ds(pl.multiple_of(j * step, step), step)
            part = jnp.dot(units, down_w[:, columns], preferred_element_type=jnp.float32)
            results[pl.ds(first, 8), :, columns] = part.astype(jnp.bfloat16).reshape(8, group, step)

        for i in range(max(first, 1), first + 8):
            back_copy(i, v).start()
        if first == 0:
            own_back.start()
    own_back.wait()
    for i in range(1, 16):
        row_copy(i).wait_send()
        back_copy(i, ahead(i)).wait()


def expert_layer(x, w_gate, w_up, w_down, collective_id):
    _, group, width = x.shape
    vmem = pl.BlockSpec(memory_space=pltpu.VMEM)
    hbm = pl.BlockSpec(memory_space=pl.ANY)
    return pl.pallas_call(
        expert_kernel,
        out_shape=jax.ShapeDtypeStruct((16, group, width), jnp.bfloat16),
        in_specs=[vmem, hbm, hbm, hbm],
        out_specs=vmem,
        scratch_shapes=[
            pltpu.VMEM(w_gate.shape, jnp.bfloat16),
            pltpu.VMEM(w_up.shape, jnp.bfloat16),
            pltpu.VMEM(w_down.shape, jnp.bfloat16),
            pltpu.VMEM((16, group, width), jnp.bfloat16),
            pltpu.VMEM((16, group, width), jnp.bfloat16),
            pltpu.SemaphoreType.DMA((3,)),
            pltpu.SemaphoreType.DMA((16,)),
            pltpu.SemaphoreType.DMA((16,)),
            pltpu.SemaphoreType.DMA((16,)),
            pltpu.SemaphoreType.DMA((16,)),
            pltpu.SemaphoreType.DMA((2,)),
        ],
        compiler_params=pltpu.CompilerParams(
            collective_id=collective_id, has_side_effects=True, vmem_limit_bytes=56 * 1024 * 1024
        ),
    )(x, w_gate, w_up, w_down)


def loss_kernel(
    rows_ref, squares_ref, ids_ref, weight_ref,
    head_own_hbm, head_pair_hbm, own_hbm, pair_hbm, student_hbm,
    loss_ref, out_ref,
    head_w, own_w, pair_w, student, expo,
    far, kept, relay, sent, final, squares, logits,
    columns_stat, stat, stats, grads, blocks, terms, landed,
    load_sem, head_send, head_recv, square_send, square_recv, stat_send, stat_recv,
    ring_send, ring_recv, term_send, term_recv, self_sem,
):
    t, v = lax.axis_index("tok"), lax.axis_index("voc")
    core = lax.rem(t, 2)
    chip = t // 2
    partner = t + 1 - 2 * core
    right, left, across = lax.rem(t + 2, 8), lax.rem(t + 6, 8), lax.rem(t + 4, 8)
    count, vocab = grads.shape
    half = count // 2
    source_core = lax.rem(v // 2, 2)
    width = own_w.shape[0]
    features = rows_ref.shape[2] * 4
    step = 256
    steps = vocab // step
    top, low = pl.ds(0, half), pl.ds(half, half)
    loads = [
        pltpu.make_async_copy(source, target, load_sem.at[i])
        for i, (source, target) in enumerate(
            (
                (head_own_hbm, head_w.at[pl.ds(pl.multiple_of(core * width, width), width)]),
                (
                    head_pair_hbm,
                    head_w.at[pl.ds(pl.multiple_of((1 - core) * width, width), width)],
                ),
                (student_hbm, student),
                (own_hbm, own_w),
                (pair_hbm, pair_w),
            )
        )
    ]
    for load in loads[:2]:
        load.start()
    barrier = pltpu.get_barrier_semaphore()
    for side in (right, left, across):
        pl.semaphore_signal(barrier, inc=1, device_id=(side, v), device_id_type=MESH)

    @pl.loop(0, 16)
    def _(k):
        pl.semaphore_signal(barrier, inc=1, device_id=(partner, k), device_id_type=MESH)

    @pl.loop(1, 16)
    def _(k):
        pl.semaphore_signal(
            barrier, inc=1, device_id=(t, lax.rem(v + k, 16)), device_id_type=MESH
        )

    pl.semaphore_wait(barrier, 34)

    chips = [lax.rem(chip + shift, 4) for shift in range(4)]
    square_copies = [
        pltpu.make_async_remote_copy(
            src_ref=squares_ref.at[chips[shift]],
            dst_ref=squares.at[shift - 1],
            send_sem=square_send.at[shift - 1],
            recv_sem=square_recv.at[shift - 1],
            device_id=(device, v),
            device_id_type=MESH,
        )
        for shift, device in ((1, right), (2, across), (3, left))
    ]
    head_plan = (
        (far.at[top], relay.at[0], right),
        (far.at[low], relay.at[1], left),
        (sent.at[0, low], final.at[0, low], right),
        (sent.at[1, top], final.at[1, top], left),
        (sent.at[0, top], final.at[0, top], right),
        (sent.at[1, low], final.at[1, low], left),
    )
    head_ring = [
        pltpu.make_async_remote_copy(
            src_ref=source,
            dst_ref=target,
            send_sem=head_send.at[i],
            recv_sem=head_recv.at[i],
            device_id=(device, v),
            device_id_type=MESH,
        )
        for i, (source, target, device) in enumerate(head_plan)
    ]
    def head_part(shift, store):
        block = rows_ref[chips[shift]]

        @pl.loop(0, steps)
        def _(j):
            columns = pl.ds(pl.multiple_of(j * step, step), step)
            store(columns, jnp.dot(block, head_w[:, columns], preferred_element_type=jnp.float32))

    def store_far(columns, value):
        far[:, columns] = value.astype(jnp.bfloat16)

    def store_right(columns, value):
        kept[0, :, columns] = value[:half]
        sent[0, low, columns] = value[half:].astype(jnp.bfloat16)

    def store_left(columns, value):
        kept[1, :, columns] = value[half:]
        sent[1, top, columns] = value[:half].astype(jnp.bfloat16)

    def store_own(columns, value):
        logits[:, columns] = value

    for load in loads[:2]:
        load.wait()
    for load in loads[2:]:
        load.start()
    head_part(2, store_far)
    head_ring[0].start()
    head_ring[1].start()
    head_part(1, store_right)
    head_ring[2].start()
    head_part(3, store_left)
    head_ring[3].start()
    for copy in square_copies:
        copy.start()
    head_part(0, store_own)
    for i, rows in ((0, top), (1, low)):
        head_ring[i].wait_recv()

        @pl.loop(0, steps)
        def _(j):
            columns = pl.ds(pl.multiple_of(j * step, step), step)
            sent[i, rows, columns] = (
                kept[i, :, columns] + relay[i, :, columns].astype(jnp.float32)
            ).astype(jnp.bfloat16)

        head_ring[4 + i].start()
    total = squares_ref[chip]
    for i, copy in enumerate(square_copies):
        copy.wait_recv()
        total += squares[i]
    inverse = lax.rsqrt(total[:, :1] / features + 1e-06)
    for load in loads[2:]:
        load.wait()
    lanes = 128
    lane = lax.broadcasted_iota(jnp.int32, (half, lanes), 1)
    start = v * vocab
    lowest = jnp.full((half, lanes), -jnp.inf, jnp.float32)
    nothing = jnp.zeros((half, lanes), jnp.float32)

    def sweep(body, carry):
        def pair(j, carry):
            for u in range(2):
                first = j * 2 * lanes + u * lanes
                carry = body(pl.ds(pl.multiple_of(first, lanes), lanes), first, carry)
            return carry

        return lax.fori_loop(0, vocab // (2 * lanes), pair, carry)

    def row_sum(value):
        return jnp.sum(value, axis=1, keepdims=True)

    student_side = []
    for part in (top, low):
        target = ids_ref[part, :][:, :1] - start
        student_max = jnp.max(
            sweep(lambda at, first, carry: jnp.maximum(carry, student[part, at]), lowest),
            axis=1,
            keepdims=True,
        )

        def student_sums(at, first, carry):
            own = student[part, at]
            weight = jnp.exp(own - student_max)
            expo[part, at] = weight
            return carry[0] + weight, carry[1] + jnp.where(lane + first == target, own, 0.0)

        total, picked = sweep(student_sums, (nothing, nothing))
        student_side.append((target, student_max, row_sum(total), row_sum(picked)))

    for i in range(2, 6):
        head_ring[i].wait_recv()

    for index, part in enumerate((top, low)):
        scale = inverse[part.start : part.start + half]
        target, student_max, student_sum, student_picked = student_side[index]

        def largest(at, first, carry):
            value = (
                logits[part, at]
                + final[0, part, at].astype(jnp.float32)
                + final[1, part, at].astype(jnp.float32)
            ) * scale
            logits[part, at] = value
            return jnp.maximum(carry, value)

        teacher_max = jnp.max(sweep(largest, lowest), axis=1, keepdims=True)

        def sums(at, first, carry):
            teacher = logits[part, at]
            return (
                carry[0] + jnp.exp(teacher - teacher_max),
                carry[1] + expo[part, at] * (student[part, at] - teacher),
                carry[2] + jnp.where(lane + first == target, teacher, 0.0),
            )

        teacher_sum, cross, teacher_picked = [
            row_sum(total) for total in sweep(sums, (nothing,) * 3)
        ]
        table = jnp.where(lane == 0, teacher_max, 0.0)
        for i, column in enumerate(
            (student_max, teacher_sum, student_sum, cross, student_picked, teacher_picked)
        ):
            table = jnp.where(lane == i + 1, column, table)
        columns_stat[part, :] = table

    stat[...] = jnp.transpose(columns_stat[...])[:8]

    def stat_copy(k, sender):
        return pltpu.make_async_remote_copy(
            src_ref=stat,
            dst_ref=stats.at[sender],
            send_sem=stat_send.at[k],
            recv_sem=stat_recv.at[k],
            device_id=(t, lax.rem(v + k, 16)),
            device_id_type=MESH,
        )

    @pl.loop(1, 16)
    def _(k):
        stat_copy(k, v).start()

    stats[v] = stat[...]

    @pl.loop(1, 16)
    def _(k):
        stat_copy(k, lax.rem(v - k + 16, 16)).wait()

    every = [stats[:, pl.ds(i, 1), :] for i in range(7)]
    teacher_max = jnp.max(every[0], axis=0)
    student_max = jnp.max(every[1], axis=0)
    teacher_sum = jnp.sum(every[2] * jnp.exp(every[0] - teacher_max), axis=0)
    student_scale = jnp.exp(every[1] - student_max)
    student_sum = jnp.sum(every[3] * student_scale, axis=0)
    expect = jnp.sum(every[4] * student_scale, axis=0) / student_sum
    teacher_norm = teacher_max + jnp.log(teacher_sum)
    student_norm = student_max + jnp.log(student_sum)
    loss_ref[...] = (
        expect
        - student_norm
        + teacher_norm
        + (jnp.sum(every[5], axis=0) - student_norm)
        - (jnp.sum(every[6], axis=0) - teacher_norm)
    )
    sublane = lax.broadcasted_iota(jnp.int32, (lanes, lanes), 0)
    columns_stat[...] = jnp.transpose(
        jnp.where(sublane == 0, student_norm, jnp.where(sublane == 1, expect, 0.0))
    )
    for index, part in enumerate((top, low)):
        norm = columns_stat[part, :][:, 0:1]
        mean = columns_stat[part, :][:, 1:2]
        scale = weight_ref[part, :][:, :1]
        target, local_max, _, _ = student_side[index]
        factor = jnp.exp(local_max - norm)

        def gradient(at, first, carry):
            prob = expo[part, at] * factor
            picked = (lane + first == target).astype(jnp.float32)
            grads[part, at] = (
                scale * (prob * (student[part, at] - logits[part, at] - mean) + picked - prob)
            ).astype(jnp.bfloat16)
            return carry

        sweep(gradient, 0)

    for copy in square_copies:
        copy.wait_send()
    for copy in head_ring:
        copy.wait_send()

    plan = (
        (grads.at[top], blocks.at[0, top], right),
        (grads.at[low], blocks.at[0, low], right),
        (grads.at[low], blocks.at[1, low], left),
        (grads.at[top], blocks.at[1, top], left),
        (blocks.at[0, top], blocks.at[2, top], right),
        (blocks.at[1, low], blocks.at[2, low], left),
    )
    ring = [
        pltpu.make_async_remote_copy(
            src_ref=source,
            dst_ref=target,
            send_sem=ring_send.at[i],
            recv_sem=ring_recv.at[i],
            device_id=(device, v),
            device_id_type=MESH,
        )
        for i, (source, target, device) in enumerate(plan)
    ]
    for i in (0, 2, 1, 3):
        ring[i].start()

    def term_copy(slot, side, h, piece):
        return pltpu.make_async_remote_copy(
            src_ref=terms.at[slot, side, pl.ds(h * half, half)],
            dst_ref=landed.at[v],
            send_sem=term_send.at[slot * 4 + side * 2 + h],
            recv_sem=term_recv.at[v],
            device_id=(partner if side else t, piece),
            device_id_type=MESH,
        )

    def self_copy(slot, h):
        return pltpu.make_async_copy(
            terms.at[slot, 0, pl.ds(h * half, half)], landed.at[v], self_sem
        )

    pieces = [
        [lax.rem(chip + shift, 4) * 4 + 2 * core + h for h in range(2)] for shift in (0, 3, 1, 2)
    ]

    def multiply(slot, block):
        for side, weight in enumerate((own_w, pair_w)):
            terms[slot, side] = lax.dot_general(
                block[...], weight[...], (((1,), (1,)), ((), ())), preferred_element_type=jnp.float32
            ).astype(jnp.bfloat16)
            for h in range(2):
                piece = pieces[slot][h]
                if side:
                    term_copy(slot, side, h, piece).start()
                else:
                    pl.when(piece != v)(term_copy(slot, side, h, piece).start)
                    pl.when(piece == v)(self_copy(slot, h).start)

    multiply(0, grads)
    ring[0].wait_recv()
    ring[4].start()
    ring[2].wait_recv()
    ring[5].start()
    ring[1].wait_recv()
    multiply(1, blocks.at[0])
    ring[3].wait_recv()
    multiply(2, blocks.at[1])
    ring[4].wait_recv()
    ring[5].wait_recv()
    multiply(3, blocks.at[2])

    for slot in range(4):
        for h in range(2):
            piece = pieces[slot][h]
            term_copy(slot, 1, h, piece).wait_send()
            pl.when(piece != v)(term_copy(slot, 0, h, piece).wait_send)
            pl.when(piece == v)(self_copy(slot, h).wait)
    for copy in ring:
        copy.wait_send()

    @pl.loop(0, 16)
    def _(k):
        @pl.when(jnp.logical_or(source_core != core, k != v))
        def _():
            pltpu.make_async_remote_copy(
                src_ref=terms.at[0, 0, top],
                dst_ref=landed.at[k],
                send_sem=term_send.at[0],
                recv_sem=term_recv.at[k],
                device_id=(partner, v),
                device_id_type=MESH,
            ).wait_recv()

    total = landed[0].astype(jnp.float32)
    for k in range(1, 16):
        total += landed[k].astype(jnp.float32)
    out_ref[...] = total.astype(out_ref.dtype)


def loss_and_grad(
    rows, squares, ids, weight, head_own, head_pair, own, pair, student, collective_id
):
    _, count, _ = rows.shape
    width, vocab = head_own.shape
    vmem = pl.BlockSpec(memory_space=pltpu.VMEM)
    hbm = pl.BlockSpec(memory_space=pl.ANY)
    bf16, f32 = jnp.bfloat16, jnp.float32
    dma = pltpu.SemaphoreType.DMA
    return pl.pallas_call(
        loss_kernel,
        out_shape=(
            jax.ShapeDtypeStruct((1, count), f32),
            jax.ShapeDtypeStruct((count // 2, width), bf16),
        ),
        in_specs=[vmem] * 4 + [hbm] * 5,
        out_specs=(vmem, vmem),
        scratch_shapes=[
            pltpu.VMEM((2 * width, vocab), bf16),
            pltpu.VMEM((width, vocab), bf16),
            pltpu.VMEM((width, vocab), bf16),
            pltpu.VMEM((count, vocab), f32),
            pltpu.VMEM((count, vocab), f32),
            pltpu.VMEM((count, vocab), bf16),
            pltpu.VMEM((2, count // 2, vocab), f32),
            pltpu.VMEM((2, count // 2, vocab), bf16),
            pltpu.VMEM((2, count, vocab), bf16),
            pltpu.VMEM((2, count, vocab), bf16),
            pltpu.VMEM((3, count, 128), f32),
            pltpu.VMEM((count, vocab), f32),
            pltpu.VMEM((count, 128), f32),
            pltpu.VMEM((8, count), f32),
            pltpu.VMEM((16, 8, count), f32),
            pltpu.VMEM((count, vocab), bf16),
            pltpu.VMEM((3, count, vocab), bf16),
            pltpu.VMEM((4, 2, count, width), bf16),
            pltpu.VMEM((16, count // 2, width), bf16),
            dma((5,)),
            dma((6,)),
            dma((6,)),
            dma((3,)),
            dma((3,)),
            dma((16,)),
            dma((16,)),
            dma((6,)),
            dma((6,)),
            dma((16,)),
            dma((16,)),
            dma,
        ],
        compiler_params=pltpu.CompilerParams(
            collective_id=collective_id, has_side_effects=True, vmem_limit_bytes=60 * 1024 * 1024
        ),
    )(rows, squares, ids, weight, head_own, head_pair, own, pair, student)


def per_device(
    tokens_in,
    gate_raw,
    expert_ids,
    w_gate,
    w_up,
    w_down,
    final_gain,
    teacher_head,
    student_hidden,
    student_head,
    sampled_ids,
    token_weight,
):
    tok_count = lax.axis_size("tok")
    voc_count = lax.axis_size("voc")
    rows_here, top_k = expert_ids.shape
    model_width = tokens_in.shape[1]
    part_width = model_width // tok_count
    student_pair = lax.ppermute(student_head, "tok", [(i, i ^ 1) for i in range(tok_count)])
    teacher_pair = lax.ppermute(teacher_head, "tok", [(i, i ^ 1) for i in range(tok_count)])
    ids_shares = jnp.concatenate(
        [expert_ids.astype(jnp.float32), gate_raw, jnp.zeros((rows_here, 128 - 2 * top_k), jnp.float32)],
        axis=1,
    )
    rows_all = tok_count * rows_here
    student_all, tokens_all, table = exchange(
        [student_hidden, tokens_in, ids_shares],
        [
            (voc_count,) + student_hidden.shape,
            (tok_count, rows_here, model_width),
            (tok_count, rows_here, 128),
        ],
        ("voc", "tok", "tok"),
        2,
        targets=(at_peer, at_core_chip, at_core_chip),
    )
    student_part = jnp.dot(
        student_all.reshape(-1, part_width), student_head, preferred_element_type=jnp.float32
    )
    tokens_all = tokens_all.reshape(rows_all, model_width)
    table = table.reshape(rows_all, 128)
    slots = 2
    here = voc_count // 2
    column = jnp.arange(here * tok_count * slots, dtype=jnp.int32)
    column_expert = column // (tok_count * slots) + lax.axis_index("tok") * here
    column_block = column // slots % tok_count
    column_slot = column % slots
    row = jnp.arange(rows_all, dtype=jnp.int32)
    gates = table[:, top_k : 2 * top_k]
    shares = gates / jnp.sum(gates, axis=1, keepdims=True)
    named = [
        table[:, k : k + 1] == column_expert.astype(jnp.float32)[None, :] for k in range(top_k)
    ]
    present = functools.reduce(jnp.logical_or, named)
    share_of = sum(jnp.where(named[k], shares[:, k : k + 1], 0.0) for k in range(top_k))
    before = (row[:, None] // rows_here == row[None, :] // rows_here) & (row[None, :] < row[:, None])
    earlier = jnp.dot(
        before.astype(jnp.bfloat16), present.astype(jnp.bfloat16), preferred_element_type=jnp.float32
    )
    matched = (
        present
        & (earlier == column_slot.astype(jnp.float32)[None, :])
        & (row[:, None] // rows_here == column_block[None, :])
    )
    combine_table = jnp.where(matched, share_of, 0.0)
    dispatched = lax.dot_general(
        matched.astype(jnp.bfloat16),
        tokens_all,
        (((0,), (0,)), ((), ())),
        preferred_element_type=jnp.float32,
    ).astype(jnp.bfloat16)
    group = tok_count * slots
    dispatched, student_part = lax.optimization_barrier((dispatched, student_part))
    student_logits = lax.psum_scatter(student_part, "tok", scatter_dimension=0, tiled=True)
    returned = expert_layer(
        dispatched.reshape(here, group, model_width), w_gate, w_up, w_down, 3
    )
    pair_sum = jnp.sum(
        returned.astype(jnp.float32).reshape(here, 2, group, model_width), axis=1
    ).reshape(here * group, model_width)
    mix_part = jnp.dot(combine_table, pair_sum, precision=lax.Precision.HIGHEST)
    core_rows, chip_width = rows_all // 2, 2 * part_width
    (mix_parts,) = exchange(
        [mix_part.astype(jnp.bfloat16)],
        [(tok_count, core_rows, chip_width)],
        ("tok",),
        6,
        source=at_core_features,
    )
    tok_index = lax.axis_index("tok")
    feature_start = (tok_index // 2) * chip_width
    tokens_part = lax.dynamic_slice(
        tokens_all, ((tok_index % 2) * core_rows, feature_start), (core_rows, chip_width)
    )
    residual_sum = tokens_part.astype(jnp.float32) + jnp.sum(mix_parts.astype(jnp.float32), axis=0)
    squares = jnp.sum(residual_sum * residual_sum, axis=1, keepdims=True)
    gain_part = lax.dynamic_slice_in_dim(final_gain, feature_start, chip_width, 0)
    scaled = (residual_sum * gain_part[None, :]).astype(jnp.bfloat16)
    chips = tok_count // 2
    teacher_rows, squares_rows = exchange(
        [
            scaled.reshape(chips, rows_here, chip_width),
            jnp.broadcast_to(squares, (core_rows, 128)).reshape(chips, rows_here, 128),
        ],
        [
            (chips, voc_count, rows_here, chip_width),
            (chips, voc_count, rows_here, 128),
        ],
        ("voc", "voc"),
        8,
        targets=(at_second, at_second),
    )
    token_count = sampled_ids.shape[0]
    token_loss, hidden_grad = loss_and_grad(
        teacher_rows.reshape(chips, token_count, chip_width),
        squares_rows.reshape(chips, token_count, 128),
        jnp.broadcast_to(sampled_ids[:, None], (token_count, 128)),
        jnp.broadcast_to(token_weight[:, None], (token_count, 128)),
        teacher_head,
        teacher_pair,
        student_head,
        student_pair,
        student_logits,
        10,
    )
    token_loss = token_loss.reshape(token_count)
    return (token_loss, hidden_grad)


def solution(mesh):
    in_specs = (
        P(("tok", "voc"), None),
        P(("tok", "voc"), None),
        P(("tok", "voc"), None),
        P(None, ("tok", "voc")),
        P(None, ("tok", "voc")),
        P(("tok", "voc"), None),
        P(),
        P("tok", "voc"),
        P("voc", "tok"),
        P("tok", "voc"),
        P("tok"),
        P("tok"),
    )
    out_specs = (P("tok"), P("voc", "tok"))
    return jax.shard_map(
        per_device, mesh=mesh, in_specs=in_specs, out_specs=out_specs, check_vma=False
    )
```

```python
import functools
import jax
import jax.numpy as jnp
from jax import lax
from jax.experimental import pallas as pl
from jax.experimental.pallas import tpu as pltpu
from jax.sharding import PartitionSpec as P

MESH = pl.DeviceIdType.MESH


def device_on(axis, index):
    if axis == "tok":
        return (index, lax.axis_index("voc"))
    return (lax.axis_index("tok"), index)


def exchange_kernel(axes, sizes, source, targets, *refs):
    count = len(axes)
    ins, outs = refs[:count], refs[count : 2 * count]
    send_sem, recv_sem, own_sem = refs[2 * count :]
    barrier = pltpu.get_barrier_semaphore()
    for axis in sorted(set(axes)):
        n = sizes[axis]

        @pl.loop(1, n)
        def _(k):
            peer = lax.rem(lax.axis_index(axis) + k, n)
            pl.semaphore_signal(barrier, inc=1, device_id=device_on(axis, peer), device_id_type=MESH)

    pl.semaphore_wait(barrier, sum(sizes[axis] - 1 for axis in set(axes)))

    def copy(i, k, back):
        me, n = lax.axis_index(axes[i]), sizes[axes[i]]
        peer = lax.rem(me + k, n)
        return pltpu.make_async_remote_copy(
            src_ref=source(ins[i], peer),
            dst_ref=targets[i](outs[i], lax.rem(me - k + n, n) if back else me),
            send_sem=send_sem.at[i, k],
            recv_sem=recv_sem.at[i, k],
            device_id=device_on(axes[i], peer),
            device_id_type=MESH,
        )

    for i in range(count):

        @pl.loop(1, sizes[axes[i]])
        def _(k):
            copy(i, k, False).start()

    for i in range(count):
        me = lax.axis_index(axes[i])
        own = pltpu.make_async_copy(source(ins[i], me), targets[i](outs[i], me), own_sem)
        own.start()
        own.wait()

    for i in range(count):

        @pl.loop(1, sizes[axes[i]])
        def _(k):
            copy(i, k, True).wait()


def whole(ref, peer):
    return ref


def at_peer(ref, peer):
    return ref.at[peer]


def at_pair(ref, peer):
    return ref.at[peer // 2]


def at_second(ref, peer):
    return ref.at[:, peer]


def at_core_chip(ref, peer):
    return ref.at[lax.rem(peer, 2) * 4 + peer // 2]


def at_core_features(ref, peer):
    rows = pl.ds(pl.multiple_of(lax.rem(peer, 2) * 32, 32), 32)
    return ref.at[rows, pl.ds(pl.multiple_of((peer // 2) * 1024, 1024), 1024)]


def exchange(arrays, shapes, axes, collective_id, source=whole, targets=None):
    count = len(arrays)
    sizes = {axis: lax.axis_size(axis) for axis in axes}
    return pl.pallas_call(
        functools.partial(
            exchange_kernel, axes, sizes, source, targets or (at_peer,) * count
        ),
        out_shape=[jax.ShapeDtypeStruct(o, x.dtype) for o, x in zip(shapes, arrays)],
        in_specs=[pl.BlockSpec(memory_space=pltpu.VMEM)] * count,
        out_specs=[pl.BlockSpec(memory_space=pltpu.VMEM)] * count,
        scratch_shapes=[
            pltpu.SemaphoreType.DMA((count, max(sizes.values()))),
            pltpu.SemaphoreType.DMA((count, max(sizes.values()))),
            pltpu.SemaphoreType.DMA,
        ],
        compiler_params=pltpu.CompilerParams(collective_id=collective_id, has_side_effects=True),
    )(*arrays)


OFFSETS = (
    (0, 1), (1, 0), (0, 3), (3, 0), (1, 1), (3, 3), (1, 3),
    (3, 1), (2, 0), (0, 2), (1, 2), (2, 1), (3, 2), (2, 3), (2, 2),
)


def expert_kernel(
    x_ref, gate_hbm, up_hbm, down_hbm, out_ref,
    gate_w, up_w, down_w, rows, results,
    load_sem, rows_send, rows_recv, back_send, back_recv, own_sem,
):
    v = lax.axis_index("voc")
    y, z = v // 4, lax.rem(v, 4)
    loads = [
        pltpu.make_async_copy(source, target, load_sem.at[i])
        for i, (source, target) in enumerate(
            ((gate_hbm, gate_w), (up_hbm, up_w), (down_hbm, down_w))
        )
    ]
    for load in loads:
        load.start()

    def ahead(i):
        dy, dz = OFFSETS[i - 1]
        return lax.rem(y + dy, 4) * 4 + lax.rem(z + dz, 4)

    def behind(i):
        dy, dz = OFFSETS[i - 1]
        return lax.rem(y + 4 - dy, 4) * 4 + lax.rem(z + 4 - dz, 4)

    barrier = pltpu.get_barrier_semaphore()
    for i in range(1, 16):
        pl.semaphore_signal(
            barrier, inc=1, device_id=device_on("voc", ahead(i)), device_id_type=MESH
        )
    pl.semaphore_wait(barrier, 15)

    def row_copy(i):
        return pltpu.make_async_remote_copy(
            src_ref=x_ref.at[ahead(i) // 2],
            dst_ref=rows.at[i],
            send_sem=rows_send.at[i],
            recv_sem=rows_recv.at[i],
            device_id=device_on("voc", ahead(i)),
            device_id_type=MESH,
        )

    def back_copy(i, place):
        return pltpu.make_async_remote_copy(
            src_ref=results.at[i],
            dst_ref=out_ref.at[place],
            send_sem=back_send.at[i],
            recv_sem=back_recv.at[i],
            device_id=device_on("voc", behind(i)),
            device_id_type=MESH,
        )

    for i in range(1, 16):
        row_copy(i).start()
    own = pltpu.make_async_copy(x_ref.at[v // 2], rows.at[0], own_sem.at[0])
    own.start()
    for load in loads:
        load.wait()
    own.wait()
    group, width = rows.shape[1:]
    step = 512
    own_back = pltpu.make_async_copy(results.at[0], out_ref.at[v], own_sem.at[1])
    for first in (0, 8):
        for i in range(max(first, 1), first + 8):
            row_copy(i).wait_recv()
        batch = rows[pl.ds(first, 8)].reshape(8 * group, width)
        gate = jnp.dot(batch, gate_w[...], preferred_element_type=jnp.float32)
        up = jnp.dot(batch, up_w[...], preferred_element_type=jnp.float32)
        units = (gate * jax.nn.sigmoid(gate) * up).astype(jnp.bfloat16)

        @pl.loop(0, width // step)
        def _(j):
            columns = pl.ds(pl.multiple_of(j * step, step), step)
            part = jnp.dot(units, down_w[:, columns], preferred_element_type=jnp.float32)
            results[pl.ds(first, 8), :, columns] = part.astype(jnp.bfloat16).reshape(8, group, step)

        for i in range(max(first, 1), first + 8):
            back_copy(i, v).start()
        if first == 0:
            own_back.start()
    own_back.wait()
    for i in range(1, 16):
        row_copy(i).wait_send()
        back_copy(i, ahead(i)).wait()


def expert_layer(x, w_gate, w_up, w_down, collective_id):
    _, group, width = x.shape
    vmem = pl.BlockSpec(memory_space=pltpu.VMEM)
    hbm = pl.BlockSpec(memory_space=pl.ANY)
    return pl.pallas_call(
        expert_kernel,
        out_shape=jax.ShapeDtypeStruct((16, group, width), jnp.bfloat16),
        in_specs=[vmem, hbm, hbm, hbm],
        out_specs=vmem,
        scratch_shapes=[
            pltpu.VMEM(w_gate.shape, jnp.bfloat16),
            pltpu.VMEM(w_up.shape, jnp.bfloat16),
            pltpu.VMEM(w_down.shape, jnp.bfloat16),
            pltpu.VMEM((16, group, width), jnp.bfloat16),
            pltpu.VMEM((16, group, width), jnp.bfloat16),
            pltpu.SemaphoreType.DMA((3,)),
            pltpu.SemaphoreType.DMA((16,)),
            pltpu.SemaphoreType.DMA((16,)),
            pltpu.SemaphoreType.DMA((16,)),
            pltpu.SemaphoreType.DMA((16,)),
            pltpu.SemaphoreType.DMA((2,)),
        ],
        compiler_params=pltpu.CompilerParams(
            collective_id=collective_id, has_side_effects=True, vmem_limit_bytes=56 * 1024 * 1024
        ),
    )(x, w_gate, w_up, w_down)


def loss_kernel(
    rows_ref, squares_ref, ids_ref, weight_ref,
    head_own_hbm, head_pair_hbm, own_hbm, pair_hbm, student_hbm,
    loss_ref, out_ref,
    head_w, own_w, pair_w, student, expo,
    far, kept, relay, sent, final, squares, logits,
    columns_stat, stat, stats, grads, blocks, terms, landed,
    load_sem, head_send, head_recv, square_send, square_recv, stat_send, stat_recv,
    ring_send, ring_recv, term_send, term_recv, self_sem,
):
    t, v = lax.axis_index("tok"), lax.axis_index("voc")
    core = lax.rem(t, 2)
    chip = t // 2
    partner = t + 1 - 2 * core
    right, left, across = lax.rem(t + 2, 8), lax.rem(t + 6, 8), lax.rem(t + 4, 8)
    count, vocab = grads.shape
    half = count // 2
    source_core = lax.rem(v // 2, 2)
    width = own_w.shape[0]
    features = rows_ref.shape[2] * 4
    step = 256
    steps = vocab // step
    top, low = pl.ds(0, half), pl.ds(half, half)
    loads = [
        pltpu.make_async_copy(source, target, load_sem.at[i])
        for i, (source, target) in enumerate(
            (
                (head_own_hbm, head_w.at[pl.ds(pl.multiple_of(core * width, width), width)]),
                (
                    head_pair_hbm,
                    head_w.at[pl.ds(pl.multiple_of((1 - core) * width, width), width)],
                ),
                (student_hbm, student),
                (own_hbm, own_w),
                (pair_hbm, pair_w),
            )
        )
    ]
    for load in loads[:2]:
        load.start()
    barrier = pltpu.get_barrier_semaphore()
    for side in (right, left, across):
        pl.semaphore_signal(barrier, inc=1, device_id=(side, v), device_id_type=MESH)

    @pl.loop(0, 16)
    def _(k):
        pl.semaphore_signal(barrier, inc=1, device_id=(partner, k), device_id_type=MESH)

    @pl.loop(1, 16)
    def _(k):
        pl.semaphore_signal(
            barrier, inc=1, device_id=(t, lax.rem(v + k, 16)), device_id_type=MESH
        )

    pl.semaphore_wait(barrier, 34)

    chips = [lax.rem(chip + shift, 4) for shift in range(4)]
    square_copies = [
        pltpu.make_async_remote_copy(
            src_ref=squares_ref.at[chips[shift]],
            dst_ref=squares.at[shift - 1],
            send_sem=square_send.at[shift - 1],
            recv_sem=square_recv.at[shift - 1],
            device_id=(device, v),
            device_id_type=MESH,
        )
        for shift, device in ((1, right), (2, across), (3, left))
    ]
    head_plan = (
        (far.at[top], relay.at[0], right),
        (far.at[low], relay.at[1], left),
        (sent.at[0, low], final.at[0, low], right),
        (sent.at[1, top], final.at[1, top], left),
        (sent.at[0, top], final.at[0, top], right),
        (sent.at[1, low], final.at[1, low], left),
    )
    head_ring = [
        pltpu.make_async_remote_copy(
            src_ref=source,
            dst_ref=target,
            send_sem=head_send.at[i],
            recv_sem=head_recv.at[i],
            device_id=(device, v),
            device_id_type=MESH,
        )
        for i, (source, target, device) in enumerate(head_plan)
    ]
    def head_part(shift, store):
        block = rows_ref[chips[shift]]

        @pl.loop(0, steps)
        def _(j):
            columns = pl.ds(pl.multiple_of(j * step, step), step)
            store(columns, jnp.dot(block, head_w[:, columns], preferred_element_type=jnp.float32))

    def store_far(columns, value):
        far[:, columns] = value.astype(jnp.bfloat16)

    def store_right(columns, value):
        kept[0, :, columns] = value[:half]
        sent[0, low, columns] = value[half:].astype(jnp.bfloat16)

    def store_left(columns, value):
        kept[1, :, columns] = value[half:]
        sent[1, top, columns] = value[:half].astype(jnp.bfloat16)

    def store_own(columns, value):
        logits[:, columns] = value

    for load in loads[:2]:
        load.wait()
    for load in loads[2:]:
        load.start()
    head_part(2, store_far)
    head_ring[0].start()
    head_ring[1].start()
    head_part(1, store_right)
    head_ring[2].start()
    head_part(3, store_left)
    head_ring[3].start()
    for copy in square_copies:
        copy.start()
    head_part(0, store_own)
    for i, rows in ((0, top), (1, low)):
        head_ring[i].wait_recv()

        @pl.loop(0, steps)
        def _(j):
            columns = pl.ds(pl.multiple_of(j * step, step), step)
            sent[i, rows, columns] = (
                kept[i, :, columns] + relay[i, :, columns].astype(jnp.float32)
            ).astype(jnp.bfloat16)

        head_ring[4 + i].start()
    total = squares_ref[chip]
    for i, copy in enumerate(square_copies):
        copy.wait_recv()
        total += squares[i]
    inverse = lax.rsqrt(total[:, :1] / features + 1e-06)
    for load in loads[2:]:
        load.wait()
    lanes = 128
    lane = lax.broadcasted_iota(jnp.int32, (half, lanes), 1)
    start = v * vocab
    lowest = jnp.full((half, lanes), -jnp.inf, jnp.float32)
    nothing = jnp.zeros((half, lanes), jnp.float32)

    def sweep(body, carry):
        def pair(j, carry):
            for u in range(2):
                first = j * 2 * lanes + u * lanes
                carry = body(pl.ds(pl.multiple_of(first, lanes), lanes), first, carry)
            return carry

        return lax.fori_loop(0, vocab // (2 * lanes), pair, carry)

    def row_sum(value):
        return jnp.sum(value, axis=1, keepdims=True)

    student_side = []
    for part in (top, low):
        target = ids_ref[part, :][:, :1] - start
        student_max = jnp.max(
            sweep(lambda at, first, carry: jnp.maximum(carry, student[part, at]), lowest),
            axis=1,
            keepdims=True,
        )

        def student_sums(at, first, carry):
            own = student[part, at]
            weight = jnp.exp(own - student_max)
            expo[part, at] = weight
            return carry[0] + weight, carry[1] + jnp.where(lane + first == target, own, 0.0)

        total, picked = sweep(student_sums, (nothing, nothing))
        student_side.append((target, student_max, row_sum(total), row_sum(picked)))

    for i in range(2, 6):
        head_ring[i].wait_recv()

    for index, part in enumerate((top, low)):
        scale = inverse[part.start : part.start + half]
        target, student_max, student_sum, student_picked = student_side[index]

        def largest(at, first, carry):
            value = (
                logits[part, at]
                + final[0, part, at].astype(jnp.float32)
                + final[1, part, at].astype(jnp.float32)
            ) * scale
            logits[part, at] = value
            return jnp.maximum(carry, value)

        teacher_max = jnp.max(sweep(largest, lowest), axis=1, keepdims=True)

        def sums(at, first, carry):
            teacher = logits[part, at]
            return (
                carry[0] + jnp.exp(teacher - teacher_max),
                carry[1] + expo[part, at] * (student[part, at] - teacher),
                carry[2] + jnp.where(lane + first == target, teacher, 0.0),
            )

        teacher_sum, cross, teacher_picked = [
            row_sum(total) for total in sweep(sums, (nothing,) * 3)
        ]
        table = jnp.where(lane == 0, teacher_max, 0.0)
        for i, column in enumerate(
            (student_max, teacher_sum, student_sum, cross, student_picked, teacher_picked)
        ):
            table = jnp.where(lane == i + 1, column, table)
        columns_stat[part, :] = table

    stat[...] = jnp.transpose(columns_stat[...])[:8]

    def stat_copy(k, sender):
        return pltpu.make_async_remote_copy(
            src_ref=stat,
            dst_ref=stats.at[sender],
            send_sem=stat_send.at[k],
            recv_sem=stat_recv.at[k],
            device_id=(t, lax.rem(v + k, 16)),
            device_id_type=MESH,
        )

    @pl.loop(1, 16)
    def _(k):
        stat_copy(k, v).start()

    stats[v] = stat[...]

    @pl.loop(1, 16)
    def _(k):
        stat_copy(k, lax.rem(v - k + 16, 16)).wait()

    every = [stats[:, pl.ds(i, 1), :] for i in range(7)]
    teacher_max = jnp.max(every[0], axis=0)
    student_max = jnp.max(every[1], axis=0)
    teacher_sum = jnp.sum(every[2] * jnp.exp(every[0] - teacher_max), axis=0)
    student_scale = jnp.exp(every[1] - student_max)
    student_sum = jnp.sum(every[3] * student_scale, axis=0)
    expect = jnp.sum(every[4] * student_scale, axis=0) / student_sum
    teacher_norm = teacher_max + jnp.log(teacher_sum)
    student_norm = student_max + jnp.log(student_sum)
    loss_ref[...] = (
        expect
        - student_norm
        + teacher_norm
        + (jnp.sum(every[5], axis=0) - student_norm)
        - (jnp.sum(every[6], axis=0) - teacher_norm)
    )
    sublane = lax.broadcasted_iota(jnp.int32, (lanes, lanes), 0)
    columns_stat[...] = jnp.transpose(
        jnp.where(sublane == 0, student_norm, jnp.where(sublane == 1, expect, 0.0))
    )
    plan = (
        (grads.at[top], blocks.at[0, top], right),
        (grads.at[low], blocks.at[0, low], right),
        (grads.at[low], blocks.at[1, low], left),
        (grads.at[top], blocks.at[1, top], left),
        (blocks.at[0, top], blocks.at[2, top], right),
        (blocks.at[1, low], blocks.at[2, low], left),
    )
    ring = [
        pltpu.make_async_remote_copy(
            src_ref=source,
            dst_ref=target,
            send_sem=ring_send.at[i],
            recv_sem=ring_recv.at[i],
            device_id=(device, v),
            device_id_type=MESH,
        )
        for i, (source, target, device) in enumerate(plan)
    ]
    for index, part in enumerate((top, low)):
        norm = columns_stat[part, :][:, 0:1]
        mean = columns_stat[part, :][:, 1:2]
        scale = weight_ref[part, :][:, :1]
        target, local_max, _, _ = student_side[index]
        factor = jnp.exp(local_max - norm)

        def gradient(at, first, carry):
            prob = expo[part, at] * factor
            picked = (lane + first == target).astype(jnp.float32)
            grads[part, at] = (
                scale * (prob * (student[part, at] - logits[part, at] - mean) + picked - prob)
            ).astype(jnp.bfloat16)
            return carry

        sweep(gradient, 0)
        for i in ((0, 3), (1, 2))[index]:
            ring[i].start()

    for copy in square_copies:
        copy.wait_send()
    for copy in head_ring:
        copy.wait_send()

    def term_copy(slot, side, h, piece):
        return pltpu.make_async_remote_copy(
            src_ref=terms.at[slot, side, pl.ds(h * half, half)],
            dst_ref=landed.at[v],
            send_sem=term_send.at[slot * 4 + side * 2 + h],
            recv_sem=term_recv.at[v],
            device_id=(partner if side else t, piece),
            device_id_type=MESH,
        )

    def self_copy(slot, h):
        return pltpu.make_async_copy(
            terms.at[slot, 0, pl.ds(h * half, half)], landed.at[v], self_sem
        )

    pieces = [
        [lax.rem(chip + shift, 4) * 4 + 2 * core + h for h in range(2)] for shift in (0, 3, 1, 2)
    ]

    def multiply(slot, block):
        for side, weight in enumerate((own_w, pair_w)):
            terms[slot, side] = lax.dot_general(
                block[...], weight[...], (((1,), (1,)), ((), ())), preferred_element_type=jnp.float32
            ).astype(jnp.bfloat16)
            for h in range(2):
                piece = pieces[slot][h]
                if side:
                    term_copy(slot, side, h, piece).start()
                else:
                    pl.when(piece != v)(term_copy(slot, side, h, piece).start)
                    pl.when(piece == v)(self_copy(slot, h).start)

    multiply(0, grads)
    ring[0].wait_recv()
    ring[4].start()
    ring[2].wait_recv()
    ring[5].start()
    ring[1].wait_recv()
    multiply(1, blocks.at[0])
    ring[3].wait_recv()
    multiply(2, blocks.at[1])
    ring[4].wait_recv()
    ring[5].wait_recv()
    multiply(3, blocks.at[2])

    for slot in range(4):
        for h in range(2):
            piece = pieces[slot][h]
            term_copy(slot, 1, h, piece).wait_send()
            pl.when(piece != v)(term_copy(slot, 0, h, piece).wait_send)
            pl.when(piece == v)(self_copy(slot, h).wait)
    for copy in ring:
        copy.wait_send()

    @pl.loop(0, 16)
    def _(k):
        @pl.when(jnp.logical_or(source_core != core, k != v))
        def _():
            pltpu.make_async_remote_copy(
                src_ref=terms.at[0, 0, top],
                dst_ref=landed.at[k],
                send_sem=term_send.at[0],
                recv_sem=term_recv.at[k],
                device_id=(partner, v),
                device_id_type=MESH,
            ).wait_recv()

    total = landed[0].astype(jnp.float32)
    for k in range(1, 16):
        total += landed[k].astype(jnp.float32)
    out_ref[...] = total.astype(out_ref.dtype)


def loss_and_grad(
    rows, squares, ids, weight, head_own, head_pair, own, pair, student, collective_id
):
    _, count, _ = rows.shape
    width, vocab = head_own.shape
    vmem = pl.BlockSpec(memory_space=pltpu.VMEM)
    hbm = pl.BlockSpec(memory_space=pl.ANY)
    bf16, f32 = jnp.bfloat16, jnp.float32
    dma = pltpu.SemaphoreType.DMA
    return pl.pallas_call(
        loss_kernel,
        out_shape=(
            jax.ShapeDtypeStruct((1, count), f32),
            jax.ShapeDtypeStruct((count // 2, width), bf16),
        ),
        in_specs=[vmem] * 4 + [hbm] * 5,
        out_specs=(vmem, vmem),
        scratch_shapes=[
            pltpu.VMEM((2 * width, vocab), bf16),
            pltpu.VMEM((width, vocab), bf16),
            pltpu.VMEM((width, vocab), bf16),
            pltpu.VMEM((count, vocab), f32),
            pltpu.VMEM((count, vocab), f32),
            pltpu.VMEM((count, vocab), bf16),
            pltpu.VMEM((2, count // 2, vocab), f32),
            pltpu.VMEM((2, count // 2, vocab), bf16),
            pltpu.VMEM((2, count, vocab), bf16),
            pltpu.VMEM((2, count, vocab), bf16),
            pltpu.VMEM((3, count, 128), f32),
            pltpu.VMEM((count, vocab), f32),
            pltpu.VMEM((count, 128), f32),
            pltpu.VMEM((8, count), f32),
            pltpu.VMEM((16, 8, count), f32),
            pltpu.VMEM((count, vocab), bf16),
            pltpu.VMEM((3, count, vocab), bf16),
            pltpu.VMEM((4, 2, count, width), bf16),
            pltpu.VMEM((16, count // 2, width), bf16),
            dma((5,)),
            dma((6,)),
            dma((6,)),
            dma((3,)),
            dma((3,)),
            dma((16,)),
            dma((16,)),
            dma((6,)),
            dma((6,)),
            dma((16,)),
            dma((16,)),
            dma,
        ],
        compiler_params=pltpu.CompilerParams(
            collective_id=collective_id, has_side_effects=True, vmem_limit_bytes=60 * 1024 * 1024
        ),
    )(rows, squares, ids, weight, head_own, head_pair, own, pair, student)


def per_device(
    tokens_in,
    gate_raw,
    expert_ids,
    w_gate,
    w_up,
    w_down,
    final_gain,
    teacher_head,
    student_hidden,
    student_head,
    sampled_ids,
    token_weight,
):
    tok_count = lax.axis_size("tok")
    voc_count = lax.axis_size("voc")
    rows_here, top_k = expert_ids.shape
    model_width = tokens_in.shape[1]
    part_width = model_width // tok_count
    student_pair = lax.ppermute(student_head, "tok", [(i, i ^ 1) for i in range(tok_count)])
    teacher_pair = lax.ppermute(teacher_head, "tok", [(i, i ^ 1) for i in range(tok_count)])
    rows_all = tok_count * rows_here
    student_all, tokens_all, ids_all, gates_all = exchange(
        [student_hidden, tokens_in, expert_ids, gate_raw],
        [
            (voc_count,) + student_hidden.shape,
            (tok_count, rows_here, model_width),
            (tok_count, rows_here, top_k),
            (tok_count, rows_here, top_k),
        ],
        ("voc", "tok", "tok", "tok"),
        2,
        targets=(at_peer, at_core_chip, at_core_chip, at_core_chip),
    )
    student_part = jnp.dot(
        student_all.reshape(-1, part_width), student_head, preferred_element_type=jnp.float32
    )
    tokens_all = tokens_all.reshape(rows_all, model_width)
    ids_all = ids_all.reshape(rows_all, top_k)
    slots = 2
    here = voc_count // 2
    column = jnp.arange(here * tok_count * slots, dtype=jnp.int32)
    column_expert = column // (tok_count * slots) + lax.axis_index("tok") * here
    column_block = column // slots % tok_count
    column_slot = column % slots
    row = jnp.arange(rows_all, dtype=jnp.int32)
    gates = gates_all.reshape(rows_all, top_k)
    shares = gates / jnp.sum(gates, axis=1, keepdims=True)
    named = [
        ids_all[:, k : k + 1] == column_expert[None, :] for k in range(top_k)
    ]
    present = functools.reduce(jnp.logical_or, named)
    share_of = sum(jnp.where(named[k], shares[:, k : k + 1], 0.0) for k in range(top_k))
    before = (row[:, None] // rows_here == row[None, :] // rows_here) & (row[None, :] < row[:, None])
    earlier = jnp.dot(
        before.astype(jnp.bfloat16), present.astype(jnp.bfloat16), preferred_element_type=jnp.float32
    )
    matched = (
        present
        & (earlier == column_slot.astype(jnp.float32)[None, :])
        & (row[:, None] // rows_here == column_block[None, :])
    )
    combine_table = jnp.where(matched, share_of, 0.0)
    dispatched = lax.dot_general(
        matched.astype(jnp.bfloat16),
        tokens_all,
        (((0,), (0,)), ((), ())),
        preferred_element_type=jnp.float32,
    ).astype(jnp.bfloat16)
    group = tok_count * slots
    dispatched, student_part = lax.optimization_barrier((dispatched, student_part))
    student_logits = lax.psum_scatter(student_part, "tok", scatter_dimension=0, tiled=True)
    returned = expert_layer(
        dispatched.reshape(here, group, model_width), w_gate, w_up, w_down, 3
    )
    pair_sum = jnp.sum(
        returned.astype(jnp.float32).reshape(here, 2, group, model_width), axis=1
    ).reshape(here * group, model_width)
    mix_part = jnp.dot(combine_table, pair_sum, precision=lax.Precision.HIGHEST)
    token_count = sampled_ids.shape[0]
    mix_part, ids_wide, weight_wide = lax.optimization_barrier(
        (
            mix_part,
            jnp.broadcast_to(sampled_ids[:, None], (token_count, 128)),
            jnp.broadcast_to(token_weight[:, None], (token_count, 128)),
        )
    )
    core_rows, chip_width = rows_all // 2, 2 * part_width
    (mix_parts,) = exchange(
        [mix_part.astype(jnp.bfloat16)],
        [(tok_count, core_rows, chip_width)],
        ("tok",),
        6,
        source=at_core_features,
    )
    tok_index = lax.axis_index("tok")
    feature_start = (tok_index // 2) * chip_width
    tokens_part = lax.dynamic_slice(
        tokens_all, ((tok_index % 2) * core_rows, feature_start), (core_rows, chip_width)
    )
    residual_sum = tokens_part.astype(jnp.float32) + jnp.sum(mix_parts.astype(jnp.float32), axis=0)
    squares = jnp.sum(residual_sum * residual_sum, axis=1, keepdims=True)
    gain_part = lax.dynamic_slice_in_dim(final_gain, feature_start, chip_width, 0)
    scaled = (residual_sum * gain_part[None, :]).astype(jnp.bfloat16)
    chips = tok_count // 2
    teacher_rows, squares_rows = exchange(
        [
            scaled.reshape(chips, rows_here, chip_width),
            jnp.broadcast_to(squares, (core_rows, 128)).reshape(chips, rows_here, 128),
        ],
        [
            (chips, voc_count, rows_here, chip_width),
            (chips, voc_count, rows_here, 128),
        ],
        ("voc", "voc"),
        8,
        targets=(at_second, at_second),
    )
    token_loss, hidden_grad = loss_and_grad(
        teacher_rows.reshape(chips, token_count, chip_width),
        squares_rows.reshape(chips, token_count, 128),
        ids_wide,
        weight_wide,
        teacher_head,
        teacher_pair,
        student_head,
        student_pair,
        student_logits,
        10,
    )
    token_loss = token_loss.reshape(token_count)
    return (token_loss, hidden_grad)


def solution(mesh):
    in_specs = (
        P(("tok", "voc"), None),
        P(("tok", "voc"), None),
        P(("tok", "voc"), None),
        P(None, ("tok", "voc")),
        P(None, ("tok", "voc")),
        P(("tok", "voc"), None),
        P(),
        P("tok", "voc"),
        P("voc", "tok"),
        P("tok", "voc"),
        P("tok"),
        P("tok"),
    )
    out_specs = (P("tok"), P("voc", "tok"))
    return jax.shard_map(
        per_device, mesh=mesh, in_specs=in_specs, out_specs=out_specs, check_vma=False
    )
```
